256 devices in a mesh: stack: 4 (over y), tile: 64 (over z, x, core).
Axes of the slice: x: 4, y: 4, z: 8, core: 2. Of those that a mesh axis runs over, the one named last changes fastest.
Arguments:
- displacement: float32 [32, 2, 512, 128], P('stack', None, 'tile'), may hold values from -6 to 6
- lens_coef: float32 [32, 2, 8], P('stack'), may hold values from -1.8 to 1.8
- stiff_class: int32 [32, 512, 128], P('stack', 'tile'), may hold values from 0 to 3
- stiff_table: float32 [4], replicated, may hold values from 0.5 to 2
- match_src: int32 [262144], P(('stack', 'tile')), may hold values from 0 to 8191
- match_owner: int32 [262144, 1], P(('stack', 'tile')), may hold values from 0 to 63; in each aligned block of 1024 rows (0 to 1023, 1024 to 2047, ...) at most 24 rows name the same one
- match_dst: int32 [262144], P(('stack', 'tile')), may hold values from 0 to 1023
- match_level: int32 [262144], P(('stack', 'tile')), may hold values from 0 to 8
- match_offset: float32 [2, 262144], P(None, ('stack', 'tile')), may hold values from -6 to 6
Outputs:
- relaxed: float32 [32, 2, 512, 128], P('stack', None, 'tile')
- lens_fit: float32 [32, 2, 8], P('stack')
The draws below stay inside these ranges and needn't reach their ends.
Inputs may be any that keep to these rules, and one draw needn't show every extreme that they name: `match_owner`: among the 1024 entries of one device's list no tile index is named more than 24 times, a bound that some block reaches. `match_level`: level 0 marks a padding entry, whose match carries no force.
All inputs are finite; a program needn't handle non-finite values.
Results may differ from the reference program's by a relative error of at most 0.0003.
Values sent between devices are 32-bit elements; how exact they have to be, the bound alone decides.
A program may use at most 64 MiB of HBM per device.

```python
import math
import jax
import jax.numpy as jnp
import numpy as np
from jax import lax

SEC_DEV = 8
ROWS_DEV = 8
COLS = 128
MATCH_DEV = 1024
LENS = 8
NCLASS = 4
ITERS = 4
SECTIONS = 32
ROWS = 512
MATCHES = 262144
CAP = 24
N_TILE = 64


def plant(result, stream_key, least, top_value):
    spot = [jax.random.randint(jax.random.fold_in(stream_key, axis), (), 0, length) for axis, length in enumerate(result.shape)]
    main_axis = result.shape.index(max(result.shape))
    beside = spot[:main_axis] + [(spot[main_axis] + 1) % result.shape[main_axis]] + spot[main_axis + 1:]
    return result.at[tuple(spot)].set(least).at[tuple(beside)].set(top_value)


def shard_levels(own_key, dims, split, least, top_value):
    loudness = 1.0
    for position, shards_of in split:
        steps = jax.random.uniform(jax.random.fold_in(jax.random.fold_in(own_key, 6), position), (shards_of,), jnp.float32, least / len(split), top_value / len(split))
        loudness = loudness * jnp.repeat(jnp.exp(steps), dims[position] // shards_of).reshape((-1,) + (1,) * (len(dims) - 1 - position))
    return loudness


def shared_out(key, own, number, rows, count, top, limit, skew):
    ranking = jax.random.permutation(key, count)
    heavy_load, usual = shares(count, rows * top, limit, skew, True), shares(count, rows * top, limit, skew, False)
    places = jnp.arange(count)

    def named(tallies, offset_by):
        used = int((tallies > 0).sum())
        fixed = max(1, used // 4)
        shifted = fixed + (places - fixed + offset_by * (used - fixed)) % max(1, count - fixed)
        return jnp.zeros((count,), jnp.int32).at[ranking[jnp.where(places < fixed, places, shifted)]].set(jnp.asarray(tallies, jnp.int32))

    tallies = jnp.where(number % 4 == 0, named(heavy_load, number // 4), named(usual, number - number // 4 - 1))
    mixed = jax.random.permutation(jax.random.fold_in(own, 3), count)
    donor, taker = mixed[0:count // 2 * 2:2], mixed[1:count // 2 * 2:2]
    slack = jnp.minimum(tallies[donor] - 1, limit - tallies[taker]) // 2
    slack = jnp.where((donor == ranking[0]) | (taker == ranking[0]) | (tallies[taker] == 0), 0, jnp.maximum(slack, 0))
    shifted = jax.random.randint(jax.random.fold_in(own, 4), (count // 2,), 0, 1 << 20) % (slack + 1)
    tallies = tallies.at[donor].add(-shifted).at[taker].add(shifted)
    labels = jnp.searchsorted(jnp.cumsum(tallies), jnp.arange(rows * top), side="right").astype(jnp.int32)
    grid = labels.reshape(top, rows).T
    grid = grid[jax.random.permutation(jax.random.fold_in(own, 1), rows)]
    offset_by = jax.random.randint(jax.random.fold_in(own, 2), (rows, 1), 0, top)
    return jnp.take_along_axis(grid, (jnp.arange(top)[None, :] + offset_by) % top, axis=1)


def shares(count, total, limit, skew, full):
    weights = [(1 << 20) // math.isqrt(standing ** skew) + 1 for standing in range(1, count + 1)]
    largest = limit if full else min(limit, max(-(-total // count), total * weights[0] // sum(weights)))
    least = 1 if total - largest >= count - 1 else 0
    holding, surplus = [largest] + [least] * (count - 1), total - largest - least * (count - 1)
    while surplus > 0:
        candidates = [i for i in range(1, count) if holding[i] < largest] or [i for i in range(1, count) if holding[i] < limit]
        pool, left = sum([weights[i] for i in candidates]), surplus
        for i in candidates:
            extra = min(limit - holding[i], max(1, left * weights[i] // pool), surplus)
            holding[i] = holding[i] + extra
            surplus = surplus - extra
    return np.array(holding)


def bell_draw(key, shape, deviation, bound, shards=(), kind=jnp.bfloat16):
    result = jax.random.normal(key, shape, jnp.float32) * deviation
    if len(shards) > 0:
        result = shard_levels(key, shape, shards, -0.22, 0.18) * result
    return jnp.clip(result, min=-bound, max=bound).astype(kind)


def setup_inputs(seed: int = 0) -> dict:
    key_list = jax.random.split(jax.random.key(seed), 10)
    displacement = bell_draw(key_list[0], (SECTIONS, 2, ROWS, COLS), 1.0, 6.0, ((0, 4), (2, 64)), jnp.float32)
    lens_coef = bell_draw(key_list[1], (SECTIONS, 2, LENS), 0.3, 1.8, ((0, 4),), jnp.float32)
    stiff_class = plant(jax.random.randint(key_list[2], (SECTIONS, ROWS, COLS), 0, NCLASS), jax.random.fold_in(key_list[2], 1), 0, NCLASS - 1).astype(jnp.int32)
    stiff_table = jnp.clip(jnp.exp(jax.random.uniform(key_list[3], (NCLASS,), jnp.float32, math.log(0.5), math.log(2.0))), 0.5, 2.0)
    match_src = plant(jax.random.randint(key_list[4], (MATCHES,), 0, SEC_DEV * ROWS_DEV * COLS), jax.random.fold_in(key_list[4], 1), 0, (SEC_DEV * ROWS_DEV * COLS) - 1).astype(jnp.int32)
    match_owner_keys = jax.random.split(jax.random.fold_in(key_list[5], 1), MATCHES // MATCH_DEV)
    match_owner_turns = jax.random.permutation(jax.random.fold_in(key_list[5], 3), MATCHES // MATCH_DEV)
    match_owner = jax.vmap(lambda own, number: shared_out(jax.random.fold_in(key_list[5], 2), own, number, MATCH_DEV, N_TILE, 1, CAP, 2))(match_owner_keys, match_owner_turns).reshape((MATCHES, 1))
    match_dst = plant(jax.random.randint(key_list[6], (MATCHES,), 0, ROWS_DEV * COLS), jax.random.fold_in(key_list[6], 1), 0, (ROWS_DEV * COLS) - 1).astype(jnp.int32)
    match_level = plant(jax.random.randint(key_list[7], (MATCHES,), 0, 9), jax.random.fold_in(key_list[7], 1), 0, 8).astype(jnp.int32)
    match_offset = bell_draw(key_list[8], (2, MATCHES), 1.0, 6.0, ((1, 256),), jnp.float32)
    return dict(displacement=displacement, lens_coef=lens_coef, stiff_class=stiff_class, stiff_table=stiff_table, match_src=match_src, match_owner=match_owner, match_dst=match_dst, match_level=match_level, match_offset=match_offset)


step_rate = 0.04
robust_scale = 4.0
lens_rate = 4.0


def shift_cols(field, col_step):
    edge = jnp.zeros(field.shape[:-1] + (1,), field.dtype)
    if col_step == 1:
        return jnp.concatenate([field[..., 1:], edge], axis=-1)
    if col_step == -1:
        return jnp.concatenate([edge, field[..., :-1]], axis=-1)
    return field


def spring_weights(stiff_rows):
    row_count = stiff_rows.shape[-2] - 2
    centre = stiff_rows[..., 1:row_count + 1, :]
    weights = []
    for row_step in (-1, 0, 1):
        for col_step in (-1, 0, 1):
            if row_step == 0 and col_step == 0:
                continue
            scale = 1.0 if row_step == 0 or col_step == 0 else 0.5
            beside = shift_cols(stiff_rows[..., 1 + row_step:1 + row_step + row_count, :], col_step)
            weights.append(scale * jnp.minimum(centre, beside))
    return weights


def spring_force(mesh_rows, weights):
    row_count = mesh_rows.shape[-2] - 2
    centre = mesh_rows[..., 1:row_count + 1, :]
    summed = jnp.zeros(centre.shape, jnp.float32)
    place = 0
    for row_step in (-1, 0, 1):
        for col_step in (-1, 0, 1):
            if row_step == 0 and col_step == 0:
                continue
            beside = shift_cols(mesh_rows[..., 1 + row_step:1 + row_step + row_count, :], col_step)
            summed = summed + weights[place][..., None, :, :] * (beside - centre)
            place = place + 1
    return summed


def lens_basis(row_ids, col_ids, row_total, col_total, lens_count):
    ramp = 1.0 + 2.0 * (row_ids.astype(jnp.float32) / row_total)
    degree = jnp.arange(lens_count, dtype=jnp.float32)[:, None]
    return ramp[None, :] * jnp.cos(jnp.pi * degree * (col_ids.astype(jnp.float32)[None, :] / col_total))


def lens_value(coef_slots, basis):
    return jnp.sum(coef_slots * basis[None], axis=1)


def pull_force(offset, base_weight):
    return base_weight * offset / (1.0 + jnp.sum(offset * offset, axis=0) / robust_scale)


def reference(displacement, lens_coef, stiff_class, stiff_table, match_src, match_owner, match_dst, match_level, match_offset):
    node_plane = ROWS_DEV * COLS
    match_ids = jnp.arange(MATCHES, dtype=jnp.int32)
    device_ids = match_ids // MATCH_DEV
    group_ids = device_ids // N_TILE
    tile_ids = device_ids % N_TILE
    local_sec = match_src // node_plane
    within = match_src % node_plane
    src_sec = group_ids * SEC_DEV + local_sec
    src_row = tile_ids * ROWS_DEV + within // COLS
    src_col = within % COLS
    dst_sec = jnp.minimum(src_sec + 1, SECTIONS - 1)
    dst_row = match_owner[:, 0] * ROWS_DEV + match_dst // COLS
    dst_col = match_dst % COLS
    usable = src_sec < SECTIONS - 1
    base_weight = jnp.where(usable, match_level, 0).astype(jnp.float32) * 0.125
    src_basis = lens_basis(src_row, src_col, ROWS, COLS, LENS)
    dst_basis = lens_basis(dst_row, dst_col, ROWS, COLS, LENS)
    degree = jnp.arange(LENS, dtype=jnp.float32)[:, None]
    col_table = jnp.cos(jnp.pi * degree * (jnp.arange(COLS, dtype=jnp.int32).astype(jnp.float32)[None, :] / COLS))
    ramp_rows = 1.0 + 2.0 * (jnp.arange(ROWS, dtype=jnp.int32).astype(jnp.float32) / ROWS)
    stiffness = stiff_table[stiff_class]
    lens_step = lens_rate * SEC_DEV / (MATCH_DEV * N_TILE)
    stiff_rows = jnp.pad(stiffness, ((0, 0), (1, 1), (0, 0)))
    weights = spring_weights(stiff_rows)

    def section_force(pair):
        mesh_sec, weight_sec = pair
        return spring_force(jnp.pad(mesh_sec, ((0, 0), (1, 1), (0, 0))), [w for w in weight_sec])

    mesh = displacement
    coefs = lens_coef
    weight_stack = jnp.stack(weights, axis=1)
    for sweep in range(ITERS):
        springs = lax.map(section_force, (mesh, weight_stack))
        src_pos = mesh[src_sec, :, src_row, src_col].T + lens_value(coefs[src_sec].transpose(1, 2, 0), src_basis) + match_offset
        dst_pos = mesh[dst_sec, :, dst_row, dst_col].T + lens_value(coefs[dst_sec].transpose(1, 2, 0), dst_basis)
        pulled = pull_force(src_pos - dst_pos, base_weight)
        match_force = jnp.zeros_like(mesh).at[dst_sec, :, dst_row, dst_col].add(pulled.T)
        match_force = match_force.at[src_sec, :, src_row, src_col].add(-pulled.T)
        projected = jnp.einsum("scrx,kx->scrk", match_force, col_table, precision=lax.Precision.HIGHEST)
        gradient = jnp.sum(projected * ramp_rows[None, None, :, None], axis=2)
        coefs = coefs + lens_step * gradient
        mesh = mesh + step_rate * (springs + match_force)
    return mesh, coefs
```

```python
import functools

import jax
import jax.numpy as jnp
import numpy as np
from jax import lax
from jax.experimental import pallas as pl
from jax.experimental.pallas import tpu as pltpu
from jax.sharding import PartitionSpec as P

ITERS = 4
STEP_RATE = 0.04
LENS_RATE = 4.0
MESH = pl.DeviceIdType.MESH
F32, BF16, I32 = jnp.float32, jnp.bfloat16, jnp.int32

SEC, EXT = 8, 9
TILES, STACKS = 64, 4
HALF = 12
GROW = 48
LENS = 8

NEAR = [(dx, dc) for dx in (2, 1, 3, 0) for dc in (1, 0)]
STEPS = [(dr, dc, 1.0 if dr == 0 or dc == 0 else 0.5) for dr in (-1, 0, 1) for dc in (-1, 0, 1) if dr or dc]


def iota(shape, dim):
    return lax.broadcasted_iota(I32, shape, dim)


def split(x):
    high = x.astype(BF16).astype(F32)
    return high, x - high


def rowpos(side, comp, i):
    return side * 24 + (comp * 8 + i if i < 8 else 16 + comp * 4 + i - 8)


def fold(x):
    for step in (8, 16, 32, 64):
        x = x + pltpu.roll(x, step, 1)
    return x


def pack_rows(a, b):
    last = jnp.where(iota((8, 128), 0) < 4, a[8:16], pltpu.roll(b[8:16], 4, 0))
    return jnp.concatenate([a[0:8], b[0:8], last], axis=0)


def kernel(
    disp, lens, scls, stab, msrc, mown, mdst, mlev, moff,
    dout, cout,
    D, K, W, WS, S, F, msg, box, CH, Q, rowix, offs, base, pos, tin, pull, lval, C, G, tmp, wrow,
    hs, hr, khs, khr, ys, yr, cy,
    a_send, a_recv, h_send, h_recv, k_send, k_recv, y_send, y_recv, s_send, s_recv,
):
    t = lax.axis_index("tile")
    g = lax.axis_index("stack")
    z, a = lax.div(t, 8), lax.rem(t, 8)
    x, c = lax.div(a, 2), lax.rem(a, 2)
    up_g, down_g = lax.rem(g + 1, STACKS), lax.rem(g + STACKS - 1, STACKS)
    up_t, down_t = lax.rem(t + 1, TILES), lax.rem(t + TILES - 1, TILES)

    def peer(dz, dx, dc):
        pz, px, pc = lax.rem(z + dz, 8), lax.rem(x + dx, 4), lax.rem(c + dc, 2)
        return pz * 8 + px * 2 + pc

    def each_peer(do):
        def along_z(k, carry):
            odd = lax.rem(k, 2)
            dz = 4 + lax.div(k, 2) - odd * (k)
            for dx, dc in NEAR:
                do(peer(dz, dx, dc))
            return carry

        lax.fori_loop(0, 7, along_z, 0)
        for dx, dc in NEAR:
            if dx or dc:
                do(peer(0, dx, dc))

    barrier = pltpu.get_barrier_semaphore()

    def greet(p):
        pl.semaphore_signal(barrier, inc=1, device_id={"tile": p}, device_id_type=MESH)

    each_peer(greet)
    for other in (up_g, down_g):
        pl.semaphore_signal(barrier, inc=1, device_id={"stack": other}, device_id_type=MESH)

    def send_rows(par):
        def one(p):
            pltpu.make_async_remote_copy(
                src_ref=msg.at[p], dst_ref=box.at[par, t], send_sem=a_send, recv_sem=a_recv.at[par],
                device_id={"tile": p}, device_id_type=MESH,
            ).start()

        each_peer(one)
        box[par, t] = msg[t]

    def wait_rows(par):
        got = box.at[par, pl.ds(0, TILES - 1)]
        pltpu.make_async_copy(got, got, a_recv.at[par]).wait()
        sent = msg.at[pl.ds(0, TILES - 1)]
        pltpu.make_async_copy(sent, sent, a_send).wait()

    def y_copy(src, dst, sems, recv, index, other):
        return pltpu.make_async_remote_copy(
            src_ref=src, dst_ref=dst, send_sem=sems.at[index], recv_sem=recv.at[index],
            device_id={"stack": other}, device_id_type=MESH,
        )

    def t_copy(src, dst, send, recv, other):
        return pltpu.make_async_remote_copy(
            src_ref=src, dst_ref=dst, send_sem=send, recv_sem=recv,
            device_id={"tile": other}, device_id_type=MESH,
        )

    lane8 = iota((8, 128), 1)
    sub8 = iota((8, 128), 0)
    group8 = lax.shift_right_logical(lane8, 3) - GROW // 8
    own_group = group8 == sub8

    D[0:SEC] = disp[...]
    cls = scls[...]
    stiff = jnp.zeros(cls.shape, F32)
    for k in range(4):
        stiff = jnp.where(cls == k, stab[k], stiff)
    K[0:SEC] = stiff
    C[...] = jnp.zeros_like(C)
    tmp[...] = jnp.zeros_like(tmp)
    for comp in range(2):
        tmp[:, 0:LENS] = lens[:, comp, :]
        wide = fold(tmp[...])
        C[comp : comp + 1] = jnp.sum(jnp.where(own_group, wide, 0.0), axis=0, keepdims=True)

    own = mown[...]
    tri_r, tri_c = iota((128, 256), 0), iota((128, 256), 1)
    tri = jnp.where(tri_r <= tri_c, 1.0, 0.0).astype(BF16)
    lane_own = iota((TILES, 128), 0)
    before = jnp.zeros((TILES, 128), F32)
    src, dst, lev = msrc[...], mdst[...], mlev[...]
    srow, scol = lax.shift_right_logical(src, 7), src & 127
    drow, dcol = lax.shift_right_logical(dst, 7), dst & 127
    live = jnp.where(srow + g * 64 >= STACKS * 64 - 8, 0, lev)
    ints = [v.astype(F32) for v in (srow, scol, drow, dcol, live)]
    slots = jnp.zeros((11 * 16, 128), F32)
    for j in range(8):
        own_j = own[j : j + 1]
        hot = jnp.where(lane_own == own_j, 1.0, 0.0)
        counted = jnp.dot(hot.astype(BF16), tri, preferred_element_type=F32)
        rank = jnp.sum(hot * (counted[:, :128] + before), axis=0, keepdims=True) - 1.0
        before = before + counted[:, 128:]
        rank = rank.astype(I32)
        high = jnp.where(rank >= HALF, 1, 0)
        row_hot = iota((16, 128), 0) == rank - HALF * high
        slot_hot = jnp.where(iota((128, 128), 0) == own_j + TILES * high, 1.0, 0.0).astype(BF16)
        values = [v[j : j + 1] for v in ints]
        for comp in range(2):
            off = moff[comp : comp + 1, j * 128 : (j + 1) * 128]
            first, rest = split(off)
            second, third = split(rest)
            values += [first, second, third]
        picked = jnp.concatenate([jnp.where(row_hot, v, 0.0) for v in values], axis=0).astype(BF16)
        slots = slots + lax.dot_general(picked, slot_hot, (((1,), (1,)), ((), ())), preferred_element_type=F32)
    sl = [slots[16 * v : 16 * v + 16] for v in range(11)]
    mine = sl[0:5] + [sl[5] + sl[6] + sl[7], sl[8] + sl[9] + sl[10]]

    tin[...] = jnp.zeros_like(tin)
    tin[0:112] = jnp.concatenate(mine, axis=0)
    turned = tin[...].T
    msg[:, 0, :] = turned[0:TILES]
    msg[:, 1, :] = turned[TILES:]

    pl.semaphore_wait(barrier, TILES - 1 + 2)
    first = [
        y_copy(D.at[0], D.at[SEC], s_send, s_recv, 0, down_g),
        y_copy(K.at[0], K.at[SEC], s_send, s_recv, 1, down_g),
        y_copy(C, cy, s_send, s_recv, 2, down_g),
    ]
    for copy in first:
        copy.start()
    send_rows(0)

    peer_row = (iota((16, 128), 1) & (TILES - 1)) * 8
    own_row0 = t * 8

    def side_tables(side, values):
        sr, sc, dr, dc, level = [v.astype(I32) for v in values[0:5]]
        ox, oy = values[5], values[6]
        sign = 1.0 if side == 0 else -1.0
        s_in, sec = sr & 7, lax.shift_right_logical(sr, 3)
        ysrc = (own_row0 if side == 0 else peer_row) + s_in
        ydst = (peer_row if side == 0 else own_row0) + dr
        ramp_s = (1.0 + ysrc.astype(F32) * (2.0 / 512)) * sign
        ramp_d = (1.0 + ydst.astype(F32) * (2.0 / 512)) * -sign
        offs[24 * side : 24 * side + 24] = pack_rows(ox, oy) * sign
        weight = values[4] * 0.125
        base[24 * side : 24 * side + 24] = pack_rows(weight, weight)
        rowix[side, 0] = sr if side == 0 else sec * 8 + 8 + dr
        rowix[side, 1] = sec
        own_col = sc if side == 0 else dc
        for i in range(HALF):
            at = slice(i * 128, (i + 1) * 128)
            CH[side, :, at] = jnp.where(iota((128, 128), 0) == own_col[i : i + 1], 1.0, 0.0).astype(BF16)
            parts = []
            for col, ramp in ((sc, ramp_s), (dc, ramp_d)):
                turn = (sub8 * col[i : i + 1]) & 255
                high, low = split(jnp.cos(turn.astype(F32) * (np.pi / 128)) * ramp[i : i + 1])
                parts += [high, high, low]
            Q[side, :, at] = jnp.concatenate(parts, axis=0).astype(BF16)

    side_tables(0, mine)
    cos_k = (lane8 - GROW) & 7
    col128 = iota((128, 128), 0)
    k128 = (iota((128, 128), 1) - GROW) & 7
    turn = (col128 * k128) & 255
    cos_hi, cos_lo = split(jnp.cos(turn.astype(F32) * (np.pi / 128)))
    cos_cat = jnp.concatenate([cos_hi, cos_hi, cos_lo], axis=0).astype(BF16)

    for copy in first:
        copy.wait()
    for comp in range(2):
        C[comp : comp + 1] = C[comp : comp + 1] + jnp.where(
            group8[0:1] == SEC, pltpu.roll(cy[comp : comp + 1], LENS * SEC, 1), 0.0
        )
    hs[...] = jnp.zeros_like(hs)
    khs[...] = jnp.zeros_like(khs)

    def beside(par):
        return [
            t_copy(hs.at[par, 0], hr.at[par, 1], h_send.at[par, 0], h_recv.at[par, 1], down_t),
            t_copy(hs.at[par, 1], hr.at[par, 0], h_send.at[par, 1], h_recv.at[par, 0], up_t),
        ]

    def send_beside(par):
        for s in range(EXT):
            for comp in range(2):
                r = s * 2 + comp
                hs[par, 0, r : r + 1] = D[s, comp, 0:1]
                hs[par, 1, r : r + 1] = D[s, comp, 7:8]
        for copy in beside(par):
            copy.start()

    for s in range(EXT):
        khs[0, s : s + 1] = K[s, 0:1]
        khs[1, s : s + 1] = K[s, 7:8]
    kcopies = [
        t_copy(khs.at[0], khr.at[1], k_send.at[0], k_recv.at[1], down_t),
        t_copy(khs.at[1], khr.at[0], k_send.at[1], k_recv.at[0], up_t),
    ]
    for copy in kcopies:
        copy.start()
    send_beside(0)

    def shifted(v, low, high):
        above = jnp.where(sub8 == 0, low, pltpu.roll(v, 1, 0))
        below = jnp.where(sub8 == 7, high, pltpu.roll(v, 7, 0))
        for dr, row in ((-1, above), (0, v), (1, below)):
            for dc in (-1, 0, 1):
                if dr or dc:
                    yield row if dc == 0 else pltpu.roll(row, 1 if dc < 0 else 127, 1)

    for copy in kcopies:
        copy.wait()
    has_low, has_high = jnp.where(t > 0, 1.0, 0.0), jnp.where(t < TILES - 1, 1.0, 0.0)
    for s in range(EXT):
        v = K[s]
        total = jnp.zeros((8, 128), F32)
        near = shifted(v, khr[0, s : s + 1] * has_low, khr[1, s : s + 1] * has_high)
        for n, ((dr, dc, scale), other) in enumerate(zip(STEPS, near)):
            w = scale * jnp.minimum(v, other)
            if dc:
                w = jnp.where(lane8 == (0 if dc < 0 else 127), 0.0, w)
            W[n, s] = w
            total = total + w
        WS[s] = total

    def turn_rows(par):
        both = jnp.concatenate([box[par, :, 0, :], box[par, :, 1, :]], axis=0)
        return both, both.T

    wait_rows(0)
    _, theirs = turn_rows(0)
    side_tables(1, [theirs[16 * v : 16 * v + 16] for v in range(7)])
    tin[...] = jnp.zeros_like(tin)
    G[...] = jnp.zeros_like(G)
    wrow[...] = jnp.zeros_like(wrow)

    ramp8 = 1.0 + (own_row0 + sub8).astype(F32) * (2.0 / 512)
    lens_step = LENS_RATE * SEC / (1024 * TILES)

    def gather():
        d_hi, d_lo = split(D[...].reshape(EXT * 16, 128))
        both = jnp.concatenate([d_hi, d_lo], axis=1).astype(BF16)
        for side in range(2):
            for n in range(HALF // 2):
                hot = CH[side, :, n * 256 : (n + 1) * 256]
                got = jnp.dot(both, jnp.concatenate([hot, hot], axis=0), preferred_element_type=F32)
                for m in range(2):
                    i = 2 * n + m
                    row = rowix[side, 0, i : i + 1]
                    sec, within = lax.shift_right_logical(row, 3), row & 7
                    at = slice(m * 128, (m + 1) * 128)
                    total = [jnp.zeros((8, 128), F32), jnp.zeros((8, 128), F32)]
                    for s in range(EXT):
                        hit = sec == s
                        for comp in range(2):
                            r = (s * 2 + comp) * 8
                            total[comp] = jnp.where(hit, got[r : r + 8, at], total[comp])
                    for comp in range(2):
                        value = jnp.sum(jnp.where(sub8 == within, total[comp], 0.0), axis=0, keepdims=True)
                        r = rowpos(side, comp, i)
                        tin[r : r + 1] = value

    def exchange(par):
        turned = tin[...].T
        for comp in range(2):
            msg[:, comp, :] = turned[comp * TILES : (comp + 1) * TILES] + G[comp : comp + 1]
        send_rows(par)

    def take_gradient(both):
        for comp in range(2):
            total = jnp.sum(both[comp * TILES : (comp + 1) * TILES], axis=0, keepdims=True)
            C[comp : comp + 1] = C[comp : comp + 1] + lens_step * jnp.where(group8[0:1] >= 0, total, 0.0)

    def lens_values():
        rows = []
        for comp in range(2):
            wide = jnp.broadcast_to(C[comp : comp + 1], (8, 128))
            s_hi, s_lo = split(fold(jnp.where(own_group, wide, 0.0)))
            d_hi, d_lo = split(fold(jnp.where(group8 == sub8 + 1, wide, 0.0)))
            block = lax.shift_right_logical(lane8, 3)
            row = jnp.where(block == 1, s_lo, s_hi)
            row = jnp.where(block >= 3, d_hi, row)
            rows.append(jnp.where(block == 4, d_lo, row))
        coef = jnp.concatenate(rows, axis=0)[:, 0:48].astype(BF16)
        for side in range(2):
            for n in range(HALF // 2):
                got = jnp.dot(coef, Q[side, :, n * 256 : (n + 1) * 256], preferred_element_type=F32)
                for m in range(2):
                    i = 2 * n + m
                    hit = rowix[side, 1, i : i + 1] == sub8
                    for comp in range(2):
                        r = rowpos(side, comp, i)
                        lval[r : r + 1] = jnp.sum(
                            jnp.where(hit, got[comp * 8 : comp * 8 + 8, m * 128 : (m + 1) * 128], 0.0),
                            axis=0, keepdims=True,
                        )

    def forces(theirs):
        other = jnp.concatenate([theirs[24:48], theirs[0:24]], axis=0)
        r = tin[0:48] - other + offs[...] + lval[...]
        sq = r * r
        for side in range(2):
            b = side * 24
            near = sq[b : b + 8] + sq[b + 8 : b + 16]
            last = sq[b + 16 : b + 24]
            last = last + pltpu.roll(last, 4, 0)
            size = jnp.concatenate([near, near, last], axis=0)
            pull[b : b + 24] = -base[b : b + 24] * r[b : b + 24] / (1.0 + size * 0.25)

    def scatter():
        rows72 = iota((EXT * 8, 128), 0)
        total = jnp.zeros((4 * EXT * 8, 128), F32)
        for side in range(2):
            for n in range(HALF // 2):
                cols = []
                for m in range(2):
                    i = 2 * n + m
                    hit = rows72 == rowix[side, 0, i : i + 1]
                    pieces = []
                    for comp in range(2):
                        r = rowpos(side, comp, i)
                        pieces += list(split(pull[r : r + 1]))
                    cols.append(jnp.concatenate([jnp.where(hit, p, 0.0) for p in pieces], axis=0))
                spread = jnp.concatenate(cols, axis=1).astype(BF16)
                total = total + lax.dot_general(
                    spread, CH[side, :, n * 256 : (n + 1) * 256], (((1,), (1,)), ((), ())),
                    preferred_element_type=F32,
                )
        for comp in range(2):
            b = comp * 2 * EXT * 8
            F[:, comp] = (total[b : b + EXT * 8] + total[b + EXT * 8 : b + 2 * EXT * 8]).reshape(EXT, 8, 128)

    def springs(par):
        for s in range(EXT):
            for comp in range(2):
                r = s * 2 + comp
                v = D[s, comp]
                total = -WS[s] * v
                near = shifted(v, hr[par, 0, r : r + 1], hr[par, 1, r : r + 1])
                for n, other in enumerate(near):
                    total = total + W[n, s] * other
                S[s, comp] = total

    def gradient():
        for s in range(EXT):
            for comp in range(2):
                r = comp * 16 + s
                wrow[r : r + 1] = jnp.sum(ramp8 * F[s, comp], axis=0, keepdims=True)
        w_hi, w_lo = split(wrow[...])
        cat = jnp.concatenate([w_hi, w_lo, w_hi], axis=1).astype(BF16)
        out = jnp.dot(cat, cos_cat, preferred_element_type=F32)
        group16 = lax.shift_right_logical(iota((16, 128), 1), 3) - GROW // 8
        mask = (group16 == iota((16, 128), 0)) & (group16 < EXT)
        for comp in range(2):
            G[comp : comp + 1] = jnp.sum(
                jnp.where(mask, out[comp * 16 : comp * 16 + 16], 0.0), axis=0, keepdims=True
            )

    def sweep(it, carry):
        par = lax.rem(it + 1, 2)
        hpar = lax.rem(it, 2)
        gather()
        exchange(par)
        for copy in beside(hpar):
            copy.wait()
        springs(hpar)
        wait_rows(par)
        both, theirs = turn_rows(par)
        take_gradient(both)
        lens_values()
        forces(theirs)
        scatter()
        ys[hpar, 0] = F[SEC]
        ys[hpar, 1] = F[0]
        copies = [
            t_like(hpar, 0, up_g),
            t_like(hpar, 1, down_g),
        ]
        for copy in copies:
            copy.start()
        for copy in copies:
            copy.wait()
        F[0] = F[0] + yr[hpar, 0]
        F[SEC] = F[SEC] + yr[hpar, 1]
        gradient()
        D[...] = D[...] + STEP_RATE * (S[...] + F[...])
        send_beside(1 - hpar)
        return carry

    def t_like(par, way, other):
        return pltpu.make_async_remote_copy(
            src_ref=ys.at[par, way], dst_ref=yr.at[par, way], send_sem=y_send.at[par, way],
            recv_sem=y_recv.at[par, way], device_id={"stack": other}, device_id_type=MESH,
        )

    lax.fori_loop(0, ITERS, sweep, 0)
    dout[...] = D[0:SEC]
    last = (ITERS + 1) % 2
    exchange(last)
    for copy in beside(ITERS % 2):
        copy.wait()
    wait_rows(last)
    both = jnp.concatenate([box[last, :, 0, :], box[last, :, 1, :]], axis=0)
    take_gradient(both)
    for comp in range(2):
        wide = fold(jnp.where(own_group, jnp.broadcast_to(C[comp : comp + 1], (8, 128)), 0.0))
        cout[:, comp, :] = wide[:, 0:LENS]


def on_device(displacement, lens_coef, stiff_class, stiff_table, match_src, match_owner, match_dst, match_level, match_offset):
    vmem = pl.BlockSpec(memory_space=pltpu.VMEM)
    smem = pl.BlockSpec(memory_space=pltpu.SMEM)
    V, DMA = pltpu.VMEM, pltpu.SemaphoreType.DMA
    lists = [a.reshape(8, 128) for a in (match_src, match_owner, match_dst, match_level)]
    scratch = [
        V((EXT, 2, 8, 128), F32),
        V((EXT, 8, 128), F32),
        V((8, EXT, 8, 128), F32),
        V((EXT, 8, 128), F32),
        V((EXT, 2, 8, 128), F32),
        V((EXT, 2, 8, 128), F32),
        V((TILES, 2, 128), F32),
        V((2, TILES, 2, 128), F32),
        V((2, 128, HALF * 128), BF16),
        V((2, 48, HALF * 128), BF16),
        V((2, 2, 16, 128), I32),
        V((48, 128), F32),
        V((48, 128), F32),
        V((48, 128), F32),
        V((128, 128), F32),
        V((48, 128), F32),
        V((48, 128), F32),
        V((8, 128), F32),
        V((8, 128), F32),
        V((8, 128), F32),
        V((32, 128), F32),
        V((2, 2, 24, 128), F32),
        V((2, 2, 24, 128), F32),
        V((2, 16, 128), F32),
        V((2, 16, 128), F32),
        V((2, 2, 2, 8, 128), F32),
        V((2, 2, 2, 8, 128), F32),
        V((8, 128), F32),
        DMA, DMA((2,)), DMA((2, 2)), DMA((2, 2)), DMA((2,)), DMA((2,)), DMA((2, 2)), DMA((2, 2)), DMA((3,)), DMA((3,)),
    ]
    return pl.pallas_call(
        kernel,
        out_shape=(
            jax.ShapeDtypeStruct((SEC, 2, 8, 128), F32),
            jax.ShapeDtypeStruct((SEC, 2, LENS), F32),
        ),
        in_specs=[vmem, vmem, vmem, smem] + [vmem] * 5,
        out_specs=(vmem, vmem),
        scratch_shapes=scratch,
        compiler_params=pltpu.CompilerParams(
            collective_id=0, has_side_effects=True, vmem_limit_bytes=32 * 1024 * 1024
        ),
        name="relax",
    )(displacement, lens_coef, stiff_class, stiff_table, *lists, match_offset)


def solution(mesh):
    in_specs = (
        P("stack", None, "tile", None),
        P("stack", None, None),
        P("stack", "tile", None),
        P(),
        P(("stack", "tile")),
        P(("stack", "tile"), None),
        P(("stack", "tile")),
        P(("stack", "tile")),
        P(None, ("stack", "tile")),
    )
    out_specs = (P("stack", None, "tile", None), P("stack", None, None))
    return jax.shard_map(on_device, mesh=mesh, in_specs=in_specs, out_specs=out_specs, check_vma=False)
```

```python
import functools

import jax
import jax.numpy as jnp
import numpy as np
from jax import lax
from jax.experimental import pallas as pl
from jax.experimental.pallas import tpu as pltpu
from jax.sharding import PartitionSpec as P

ITERS = 4
STEP_RATE = 0.04
LENS_RATE = 4.0
MESH = pl.DeviceIdType.MESH
F32, BF16, I32 = jnp.float32, jnp.bfloat16, jnp.int32

SEC, EXT = 8, 9
TILES, STACKS = 64, 4
HALF = 12
GROW = 48
LENS = 8

NEAR = [(dx, dc) for dx in (2, 1, 3, 0) for dc in (1, 0)]
STEPS = [(dr, dc, 1.0 if dr == 0 or dc == 0 else 0.5) for dr in (-1, 0, 1) for dc in (-1, 0, 1) if dr or dc]


def iota(shape, dim):
    return lax.broadcasted_iota(I32, shape, dim)


def split(x):
    high = x.astype(BF16).astype(F32)
    return high, x - high


def rowpos(side, comp, i):
    return side * 24 + (comp * 8 + i if i < 8 else 16 + comp * 4 + i - 8)


def fold(x):
    for step in (8, 16, 32, 64):
        x = x + pltpu.roll(x, step, 1)
    return x


def pack_rows(a, b):
    last = jnp.where(iota((8, 128), 0) < 4, a[8:16], pltpu.roll(b[8:16], 4, 0))
    return jnp.concatenate([a[0:8], b[0:8], last], axis=0)


def kernel(
    disp_in, lens_in, scls_in, stab_in, msrc_in, mown_in, mdst_in, mlev_in, moff_in,
    dout, cout,
    lens, scls, stab, msrc, mown, mdst, mlev, moff,
    D, K, W, WS, S, F, msg, box, CH, Q, rowix, offs, base, tin, pull, lval, C, G, tmp, wrow,
    hs, hr, khs, khr, ys, yr, cy,
    in_sem, a_send, a_recv, h_send, h_recv, k_send, k_recv, y_send, y_recv, s_send, s_recv,
):
    t = lax.axis_index("tile")
    g = lax.axis_index("stack")
    z, a = lax.div(t, 8), lax.rem(t, 8)
    x, c = lax.div(a, 2), lax.rem(a, 2)
    up_g, down_g = lax.rem(g + 1, STACKS), lax.rem(g + STACKS - 1, STACKS)
    up_t, down_t = lax.rem(t + 1, TILES), lax.rem(t + TILES - 1, TILES)

    def peer(dz, dx, dc):
        pz, px, pc = lax.rem(z + dz, 8), lax.rem(x + dx, 4), lax.rem(c + dc, 2)
        return pz * 8 + px * 2 + pc

    def each_peer(do):
        def along_z(k, carry):
            odd = lax.rem(k, 2)
            dz = 4 + lax.div(k, 2) - odd * (k)
            for dx, dc in NEAR:
                do(peer(dz, dx, dc))
            return carry

        lax.fori_loop(0, 7, along_z, 0)
        for dx, dc in NEAR:
            if dx or dc:
                do(peer(0, dx, dc))

    loads = [
        pltpu.make_async_copy(src, dst, in_sem.at[n])
        for n, (src, dst) in enumerate((
            (mown_in, mown), (msrc_in, msrc), (mdst_in, mdst), (mlev_in, mlev), (moff_in, moff),
            (disp_in, D.at[pl.ds(0, SEC)]), (scls_in, scls), (lens_in, lens), (stab_in, stab),
        ))
    ]
    for copy in loads:
        copy.start()
    barrier = pltpu.get_barrier_semaphore()

    def greet(p):
        pl.semaphore_signal(barrier, inc=1, device_id={"tile": p}, device_id_type=MESH)

    each_peer(greet)
    for other in (up_g, down_g):
        pl.semaphore_signal(barrier, inc=1, device_id={"stack": other}, device_id_type=MESH)

    def send_rows(par):
        def one(p):
            pltpu.make_async_remote_copy(
                src_ref=msg.at[p], dst_ref=box.at[par, t], send_sem=a_send, recv_sem=a_recv.at[par],
                device_id={"tile": p}, device_id_type=MESH,
            ).start()

        each_peer(one)
        box[par, t] = msg[t]

    def wait_rows(par):
        got = box.at[par, pl.ds(0, TILES - 1)]
        pltpu.make_async_copy(got, got, a_recv.at[par]).wait()
        sent = msg.at[pl.ds(0, TILES - 1)]
        pltpu.make_async_copy(sent, sent, a_send).wait()

    def y_copy(src, dst, sems, recv, index, other):
        return pltpu.make_async_remote_copy(
            src_ref=src, dst_ref=dst, send_sem=sems.at[index], recv_sem=recv.at[index],
            device_id={"stack": other}, device_id_type=MESH,
        )

    def t_copy(src, dst, send, recv, other):
        return pltpu.make_async_remote_copy(
            src_ref=src, dst_ref=dst, send_sem=send, recv_sem=recv,
            device_id={"tile": other}, device_id_type=MESH,
        )

    lane8 = iota((8, 128), 1)
    sub8 = iota((8, 128), 0)
    group8 = lax.shift_right_logical(lane8, 3) - GROW // 8
    own_group = group8 == sub8

    for copy in loads[0:5]:
        copy.wait()
    own = mown[...]
    tri_r, tri_c = iota((128, 256), 0), iota((128, 256), 1)
    tri = jnp.where(tri_r <= tri_c, 1.0, 0.0).astype(BF16)
    lane_own = iota((TILES, 128), 0)
    before = jnp.zeros((TILES, 128), F32)
    src, dst, lev = msrc[...], mdst[...], mlev[...]
    srow, scol = lax.shift_right_logical(src, 7), src & 127
    drow, dcol = lax.shift_right_logical(dst, 7), dst & 127
    live = jnp.where(srow + g * 64 >= STACKS * 64 - 8, 0, lev)
    ints = [v.astype(F32) for v in (srow, scol, drow, dcol, live)]
    slots = jnp.zeros((11 * 16, 128), F32)
    for j in range(8):
        own_j = own[j : j + 1]
        hot = jnp.where(lane_own == own_j, 1.0, 0.0)
        counted = jnp.dot(hot.astype(BF16), tri, preferred_element_type=F32)
        rank = jnp.sum(hot * (counted[:, :128] + before), axis=0, keepdims=True) - 1.0
        before = before + counted[:, 128:]
        rank = rank.astype(I32)
        high = jnp.where(rank >= HALF, 1, 0)
        row_hot = iota((16, 128), 0) == rank - HALF * high
        slot_hot = jnp.where(iota((128, 128), 0) == own_j + TILES * high, 1.0, 0.0).astype(BF16)
        values = [v[j : j + 1] for v in ints]
        for comp in range(2):
            off = moff[comp : comp + 1, j * 128 : (j + 1) * 128]
            first, rest = split(off)
            second, third = split(rest)
            values += [first, second, third]
        picked = jnp.concatenate([jnp.where(row_hot, v, 0.0) for v in values], axis=0).astype(BF16)
        slots = slots + lax.dot_general(picked, slot_hot, (((1,), (1,)), ((), ())), preferred_element_type=F32)
    sl = [slots[16 * v : 16 * v + 16] for v in range(11)]
    mine = sl[0:5] + [sl[5] + sl[6] + sl[7], sl[8] + sl[9] + sl[10]]

    tin[...] = jnp.zeros_like(tin)
    tin[0:112] = jnp.concatenate(mine, axis=0)
    turned = tin[...].T
    msg[:, 0, :] = turned[0:TILES]
    msg[:, 1, :] = turned[TILES:]

    pl.semaphore_wait(barrier, TILES - 1 + 2)
    send_rows(0)

    for copy in loads[5:]:
        copy.wait()
    cls = scls[...]
    stiff = jnp.zeros(cls.shape, F32)
    for k in range(4):
        stiff = jnp.where(cls == k, stab[k], stiff)
    K[0:SEC] = stiff
    C[...] = jnp.zeros_like(C)
    tmp[...] = jnp.zeros_like(tmp)
    for comp in range(2):
        tmp[:, 0:LENS] = lens[:, comp, :]
        wide = fold(tmp[...])
        C[comp : comp + 1] = jnp.sum(jnp.where(own_group, wide, 0.0), axis=0, keepdims=True)

    first = [
        y_copy(D.at[0], D.at[SEC], s_send, s_recv, 0, down_g),
        y_copy(K.at[0], K.at[SEC], s_send, s_recv, 1, down_g),
        y_copy(C, cy, s_send, s_recv, 2, down_g),
    ]
    for copy in first:
        copy.start()

    peer_row = (iota((16, 128), 1) & (TILES - 1)) * 8
    own_row0 = t * 8

    def node_tables(side, values):
        sr, sc, dr, dc = [v.astype(I32) for v in values[0:4]]
        sec = lax.shift_right_logical(sr, 3)
        rowix[side, 0] = sr if side == 0 else sec * 8 + 8 + dr
        rowix[side, 1] = sec
        own_col = sc if side == 0 else dc
        for i in range(HALF):
            at = slice(i * 128, (i + 1) * 128)
            CH[side, :, at] = jnp.where(iota((128, 128), 0) == own_col[i : i + 1], 1.0, 0.0).astype(BF16)

    def pull_tables(side, values):
        sr, sc, dr, dc = [v.astype(I32) for v in values[0:4]]
        ox, oy = values[5], values[6]
        sign = 1.0 if side == 0 else -1.0
        s_in = sr & 7
        ysrc = (own_row0 if side == 0 else peer_row) + s_in
        ydst = (peer_row if side == 0 else own_row0) + dr
        ramp_s = (1.0 + ysrc.astype(F32) * (2.0 / 512)) * sign
        ramp_d = (1.0 + ydst.astype(F32) * (2.0 / 512)) * -sign
        offs[24 * side : 24 * side + 24] = pack_rows(ox, oy) * sign
        weight = values[4] * 0.125
        base[24 * side : 24 * side + 24] = pack_rows(weight, weight)
        for i in range(HALF):
            at = slice(i * 128, (i + 1) * 128)
            parts = []
            for col, ramp in ((sc, ramp_s), (dc, ramp_d)):
                turn = (sub8 * col[i : i + 1]) & 255
                high, low = split(jnp.cos(turn.astype(F32) * (np.pi / 128)) * ramp[i : i + 1])
                parts += [high, high, low]
            Q[side, :, at] = jnp.concatenate(parts, axis=0).astype(BF16)

    def gather(side):
        d_hi, d_lo = split(D[side : side + SEC].reshape(SEC * 16, 128))
        both = jnp.concatenate([d_hi, d_lo], axis=1).astype(BF16)
        for _ in range(1):
            for n in range(HALF // 2):
                hot = CH[side, :, n * 256 : (n + 1) * 256]
                got = jnp.dot(both, jnp.concatenate([hot, hot], axis=0), preferred_element_type=F32)
                for m in range(2):
                    i = 2 * n + m
                    row = rowix[side, 0, i : i + 1]
                    sec, within = lax.shift_right_logical(row, 3), row & 7
                    at = slice(m * 128, (m + 1) * 128)
                    total = [jnp.zeros((8, 128), F32), jnp.zeros((8, 128), F32)]
                    for s in range(SEC):
                        hit = sec == s + side
                        for comp in range(2):
                            r = (s * 2 + comp) * 8
                            total[comp] = jnp.where(hit, got[r : r + 8, at], total[comp])
                    for comp in range(2):
                        value = jnp.sum(jnp.where(sub8 == within, total[comp], 0.0), axis=0, keepdims=True)
                        r = rowpos(side, comp, i)
                        tin[r : r + 1] = value

    def exchange(par):
        turned = tin[...].T
        for comp in range(2):
            msg[:, comp, :] = turned[comp * TILES : (comp + 1) * TILES] + G[comp : comp + 1]
        send_rows(par)

    node_tables(0, mine)
    tin[...] = jnp.zeros_like(tin)
    gather(0)
    pull_tables(0, mine)
    cos_k = (lane8 - GROW) & 7
    col128 = iota((128, 128), 0)
    k128 = (iota((128, 128), 1) - GROW) & 7
    turn = (col128 * k128) & 255
    cos_hi, cos_lo = split(jnp.cos(turn.astype(F32) * (np.pi / 128)))
    cos_cat = jnp.concatenate([cos_hi, cos_hi, cos_lo], axis=0).astype(BF16)

    for copy in first:
        copy.wait()
    for comp in range(2):
        C[comp : comp + 1] = C[comp : comp + 1] + jnp.where(
            group8[0:1] == SEC, pltpu.roll(cy[comp : comp + 1], LENS * SEC, 1), 0.0
        )
    hs[...] = jnp.zeros_like(hs)
    khs[...] = jnp.zeros_like(khs)

    def beside(par):
        return [
            t_copy(hs.at[par, 0], hr.at[par, 1], h_send.at[par, 0], h_recv.at[par, 1], down_t),
            t_copy(hs.at[par, 1], hr.at[par, 0], h_send.at[par, 1], h_recv.at[par, 0], up_t),
        ]

    def send_beside(par):
        for s in range(EXT):
            for comp in range(2):
                r = s * 2 + comp
                hs[par, 0, r : r + 1] = D[s, comp, 0:1]
                hs[par, 1, r : r + 1] = D[s, comp, 7:8]
        for copy in beside(par):
            copy.start()

    for s in range(EXT):
        khs[0, s : s + 1] = K[s, 0:1]
        khs[1, s : s + 1] = K[s, 7:8]
    kcopies = [
        t_copy(khs.at[0], khr.at[1], k_send.at[0], k_recv.at[1], down_t),
        t_copy(khs.at[1], khr.at[0], k_send.at[1], k_recv.at[0], up_t),
    ]
    for copy in kcopies:
        copy.start()
    send_beside(0)

    def shifted(v, low, high):
        above = jnp.where(sub8 == 0, low, pltpu.roll(v, 1, 0))
        below = jnp.where(sub8 == 7, high, pltpu.roll(v, 7, 0))
        for dr, row in ((-1, above), (0, v), (1, below)):
            for dc in (-1, 0, 1):
                if dr or dc:
                    yield row if dc == 0 else pltpu.roll(row, 1 if dc < 0 else 127, 1)

    def turn_rows(par):
        both = jnp.concatenate([box[par, :, 0, :], box[par, :, 1, :]], axis=0)
        return both, both.T

    wait_rows(0)
    _, theirs = turn_rows(0)
    yours = [theirs[16 * v : 16 * v + 16] for v in range(7)]
    node_tables(1, yours)
    gather(1)
    G[...] = jnp.zeros_like(G)
    exchange(1)
    pull_tables(1, yours)
    for copy in kcopies:
        copy.wait()
    has_low, has_high = jnp.where(t > 0, 1.0, 0.0), jnp.where(t < TILES - 1, 1.0, 0.0)
    for s in range(EXT):
        v = K[s]
        total = jnp.zeros((8, 128), F32)
        near = shifted(v, khr[0, s : s + 1] * has_low, khr[1, s : s + 1] * has_high)
        for n, ((dr, dc, scale), other) in enumerate(zip(STEPS, near)):
            w = scale * jnp.minimum(v, other)
            if dc:
                w = jnp.where(lane8 == (0 if dc < 0 else 127), 0.0, w)
            W[n, s] = w
            total = total + w
        WS[s] = total

    wrow[...] = jnp.zeros_like(wrow)

    ramp8 = 1.0 + (own_row0 + sub8).astype(F32) * (2.0 / 512)
    lens_step = LENS_RATE * SEC / (1024 * TILES)

    def take_gradient(both):
        for comp in range(2):
            total = jnp.sum(both[comp * TILES : (comp + 1) * TILES], axis=0, keepdims=True)
            C[comp : comp + 1] = C[comp : comp + 1] + lens_step * jnp.where(group8[0:1] >= 0, total, 0.0)

    def lens_values():
        rows = []
        for comp in range(2):
            wide = jnp.broadcast_to(C[comp : comp + 1], (8, 128))
            s_hi, s_lo = split(fold(jnp.where(own_group, wide, 0.0)))
            d_hi, d_lo = split(fold(jnp.where(group8 == sub8 + 1, wide, 0.0)))
            block = lax.shift_right_logical(lane8, 3)
            row = jnp.where(block == 1, s_lo, s_hi)
            row = jnp.where(block >= 3, d_hi, row)
            rows.append(jnp.where(block == 4, d_lo, row))
        coef = jnp.concatenate(rows, axis=0)[:, 0:48].astype(BF16)
        for side in range(2):
            for n in range(HALF // 2):
                got = jnp.dot(coef, Q[side, :, n * 256 : (n + 1) * 256], preferred_element_type=F32)
                for m in range(2):
                    i = 2 * n + m
                    hit = rowix[side, 1, i : i + 1] == sub8
                    for comp in range(2):
                        r = rowpos(side, comp, i)
                        lval[r : r + 1] = jnp.sum(
                            jnp.where(hit, got[comp * 8 : comp * 8 + 8, m * 128 : (m + 1) * 128], 0.0),
                            axis=0, keepdims=True,
                        )

    def forces(theirs):
        other = jnp.concatenate([theirs[24:48], theirs[0:24]], axis=0)
        r = tin[0:48] - other + offs[...] + lval[...]
        sq = r * r
        for side in range(2):
            b = side * 24
            near = sq[b : b + 8] + sq[b + 8 : b + 16]
            last = sq[b + 16 : b + 24]
            last = last + pltpu.roll(last, 4, 0)
            size = jnp.concatenate([near, near, last], axis=0)
            pull[b : b + 24] = -base[b : b + 24] * r[b : b + 24] / (1.0 + size * 0.25)

    def scatter():
        rows = iota((SEC * 8, 128), 0)
        got = []
        for side in range(2):
            total = jnp.zeros((4 * SEC * 8, 128), F32)
            for n in range(HALF // 2):
                cols = []
                for m in range(2):
                    i = 2 * n + m
                    hit = rows == rowix[side, 0, i : i + 1] - 8 * side
                    pieces = []
                    for comp in range(2):
                        r = rowpos(side, comp, i)
                        pieces += list(split(pull[r : r + 1]))
                    cols.append(jnp.concatenate([jnp.where(hit, p, 0.0) for p in pieces], axis=0))
                spread = jnp.concatenate(cols, axis=1).astype(BF16)
                total = total + lax.dot_general(
                    spread, CH[side, :, n * 256 : (n + 1) * 256], (((1,), (1,)), ((), ())),
                    preferred_element_type=F32,
                )
            total = total.reshape(2, 2, SEC, 8, 128)
            got.append(total[:, 0] + total[:, 1])
        for comp in range(2):
            F[0, comp] = got[0][comp, 0]
            F[1:SEC, comp] = got[0][comp, 1:SEC] + got[1][comp, 0 : SEC - 1]
            F[SEC, comp] = got[1][comp, SEC - 1]

    def springs(par):
        for s in range(EXT):
            for comp in range(2):
                r = s * 2 + comp
                v = D[s, comp]
                total = -WS[s] * v
                near = shifted(v, hr[par, 0, r : r + 1], hr[par, 1, r : r + 1])
                for n, other in enumerate(near):
                    total = total + W[n, s] * other
                S[s, comp] = total

    def gradient():
        for s in range(EXT):
            for comp in range(2):
                r = comp * 16 + s
                wrow[r : r + 1] = jnp.sum(ramp8 * F[s, comp], axis=0, keepdims=True)
        w_hi, w_lo = split(wrow[...])
        cat = jnp.concatenate([w_hi, w_lo, w_hi], axis=1).astype(BF16)
        out = jnp.dot(cat, cos_cat, preferred_element_type=F32)
        group16 = lax.shift_right_logical(iota((16, 128), 1), 3) - GROW // 8
        mask = (group16 == iota((16, 128), 0)) & (group16 < EXT)
        for comp in range(2):
            G[comp : comp + 1] = jnp.sum(
                jnp.where(mask, out[comp * 16 : comp * 16 + 16], 0.0), axis=0, keepdims=True
            )

    def sweep(it, carry):
        par = lax.rem(it + 1, 2)
        hpar = lax.rem(it, 2)
        for copy in beside(hpar):
            copy.wait()
        springs(hpar)
        wait_rows(par)
        both, theirs = turn_rows(par)
        take_gradient(both)
        lens_values()
        forces(theirs)
        scatter()
        ys[hpar, 0] = F[SEC]
        ys[hpar, 1] = F[0]
        copies = [
            t_like(hpar, 0, up_g),
            t_like(hpar, 1, down_g),
        ]
        for copy in copies:
            copy.start()
        for copy in copies:
            copy.wait()
        F[0] = F[0] + yr[hpar, 0]
        F[SEC] = F[SEC] + yr[hpar, 1]
        gradient()
        D[...] = D[...] + STEP_RATE * (S[...] + F[...])

        @pl.when(it < ITERS - 1)
        def _():
            gather(0)
            gather(1)

        exchange(1 - par)
        send_beside(1 - hpar)
        return carry

    def t_like(par, way, other):
        return pltpu.make_async_remote_copy(
            src_ref=ys.at[par, way], dst_ref=yr.at[par, way], send_sem=y_send.at[par, way],
            recv_sem=y_recv.at[par, way], device_id={"stack": other}, device_id_type=MESH,
        )

    lax.fori_loop(0, ITERS, sweep, 0)
    dout[...] = D[0:SEC]
    last = (ITERS + 1) % 2
    for copy in beside(ITERS % 2):
        copy.wait()
    wait_rows(last)
    both = jnp.concatenate([box[last, :, 0, :], box[last, :, 1, :]], axis=0)
    take_gradient(both)
    for comp in range(2):
        wide = fold(jnp.where(own_group, jnp.broadcast_to(C[comp : comp + 1], (8, 128)), 0.0))
        cout[:, comp, :] = wide[:, 0:LENS]


def on_device(displacement, lens_coef, stiff_class, stiff_table, match_src, match_owner, match_dst, match_level, match_offset):
    vmem = pl.BlockSpec(memory_space=pltpu.VMEM)
    hbm = pl.BlockSpec(memory_space=pltpu.HBM)
    V, DMA = pltpu.VMEM, pltpu.SemaphoreType.DMA
    lists = [a.reshape(8, 128) for a in (match_src, match_owner, match_dst, match_level)]
    scratch = [
        V((SEC, 2, LENS), F32),
        V((SEC, 8, 128), I32),
        pltpu.SMEM((4,), F32),
        V((8, 128), I32), V((8, 128), I32), V((8, 128), I32), V((8, 128), I32),
        V((2, 1024), F32),
        V((EXT, 2, 8, 128), F32),
        V((EXT, 8, 128), F32),
        V((8, EXT, 8, 128), F32),
        V((EXT, 8, 128), F32),
        V((EXT, 2, 8, 128), F32),
        V((EXT, 2, 8, 128), F32),
        V((TILES, 2, 128), F32),
        V((2, TILES, 2, 128), F32),
        V((2, 128, HALF * 128), BF16),
        V((2, 48, HALF * 128), BF16),
        V((2, 2, 16, 128), I32),
        V((48, 128), F32),
        V((48, 128), F32),
        V((128, 128), F32),
        V((48, 128), F32),
        V((48, 128), F32),
        V((8, 128), F32),
        V((8, 128), F32),
        V((8, 128), F32),
        V((32, 128), F32),
        V((2, 2, 24, 128), F32),
        V((2, 2, 24, 128), F32),
        V((2, 16, 128), F32),
        V((2, 16, 128), F32),
        V((2, 2, 2, 8, 128), F32),
        V((2, 2, 2, 8, 128), F32),
        V((8, 128), F32),
        DMA((9,)), DMA, DMA((2,)), DMA((2, 2)), DMA((2, 2)), DMA((2,)), DMA((2,)), DMA((2, 2)), DMA((2, 2)), DMA((3,)), DMA((3,)),
    ]
    return pl.pallas_call(
        kernel,
        out_shape=(
            jax.ShapeDtypeStruct((SEC, 2, 8, 128), F32),
            jax.ShapeDtypeStruct((SEC, 2, LENS), F32),
        ),
        in_specs=[hbm] * 9,
        out_specs=(vmem, vmem),
        scratch_shapes=scratch,
        compiler_params=pltpu.CompilerParams(
            collective_id=0, has_side_effects=True
        ),
        name="relax",
    )(displacement, lens_coef, stiff_class, stiff_table, *lists, match_offset)


def solution(mesh):
    in_specs = (
        P("stack", None, "tile", None),
        P("stack", None, None),
        P("stack", "tile", None),
        P(),
        P(("stack", "tile")),
        P(("stack", "tile"), None),
        P(("stack", "tile")),
        P(("stack", "tile")),
        P(None, ("stack", "tile")),
    )
    out_specs = (P("stack", None, "tile", None), P("stack", None, None))
    return jax.shard_map(on_device, mesh=mesh, in_specs=in_specs, out_specs=out_specs, check_vma=False)
```

```python
import functools

import jax
import jax.numpy as jnp
import numpy as np
from jax import lax
from jax.experimental import pallas as pl
from jax.experimental.pallas import tpu as pltpu
from jax.sharding import PartitionSpec as P

ITERS = 4
STEP_RATE = 0.04
LENS_RATE = 4.0
MESH = pl.DeviceIdType.MESH
F32, BF16, I32 = jnp.float32, jnp.bfloat16, jnp.int32

SEC, EXT = 8, 9
TILES, STACKS = 64, 4
HALF = 12
GROW = 48
LENS = 8

NEAR = [(dx, dc) for dx in (2, 1, 3, 0) for dc in (1, 0)]
STEPS = [(dr, dc, 1.0 if dr == 0 or dc == 0 else 0.5) for dr in (-1, 0, 1) for dc in (-1, 0, 1) if dr or dc]


def iota(shape, dim):
    return lax.broadcasted_iota(I32, shape, dim)


def split(x):
    high = x.astype(BF16).astype(F32)
    return high, x - high


def rowpos(side, comp, i):
    return side * 24 + (comp * 8 + i if i < 8 else 16 + comp * 4 + i - 8)


def fold(x):
    for step in (8, 16, 32, 64):
        x = x + pltpu.roll(x, step, 1)
    return x


def along_lanes(source, lanes):
    dims = lax.GatherDimensionNumbers(
        offset_dims=(), collapsed_slice_dims=(1,), start_index_map=(1,),
        operand_batching_dims=(0,), start_indices_batching_dims=(0,),
    )
    return lax.gather(
        source, lanes[:, :, None], dims, slice_sizes=(1, 1), mode=lax.GatherScatterMode.PROMISE_IN_BOUNDS
    )


def pack_rows(a, b):
    last = jnp.where(iota((8, 128), 0) < 4, a[8:16], pltpu.roll(b[8:16], 4, 0))
    return jnp.concatenate([a[0:8], b[0:8], last], axis=0)


def kernel(
    disp_in, lens_in, scls_in, stab_in, msrc_in, mown_in, mdst_in, mlev_in, moff_in,
    dout, cout,
    lens, scls, stab, msrc, mown, mdst, mlev, moff,
    D, K, W, WS, S, F, msg, box, gmsg, ebox, CH, COS, L, rowix, slotix, ramps, offs, base, tin, pull, lval, C, G, tmp, wrow,
    hs, hr, khs, khr, ys, yr, cy,
    in_sem, a_send, a_recv, h_send, h_recv, k_send, k_recv, y_send, y_recv, s_send, s_recv, e_send, e_recv,
):
    t = lax.axis_index("tile")
    g = lax.axis_index("stack")
    z, a = lax.div(t, 8), lax.rem(t, 8)
    x, c = lax.div(a, 2), lax.rem(a, 2)
    up_g, down_g = lax.rem(g + 1, STACKS), lax.rem(g + STACKS - 1, STACKS)
    up_t, down_t = lax.rem(t + 1, TILES), lax.rem(t + TILES - 1, TILES)

    def peer(dz, dx, dc):
        pz, px, pc = lax.rem(z + dz, 8), lax.rem(x + dx, 4), lax.rem(c + dc, 2)
        return pz * 8 + px * 2 + pc

    def each_peer(do):
        def along_z(k, carry):
            odd = lax.rem(k, 2)
            dz = 4 + lax.div(k, 2) - odd * (k)
            for dx, dc in NEAR:
                do(peer(dz, dx, dc))
            return carry

        lax.fori_loop(0, 7, along_z, 0)
        for dx, dc in NEAR:
            if dx or dc:
                do(peer(0, dx, dc))

    loads = [
        pltpu.make_async_copy(src, dst, in_sem.at[n])
        for n, (src, dst) in enumerate((
            (mown_in, mown), (msrc_in, msrc), (mdst_in, mdst), (mlev_in, mlev), (moff_in, moff),
            (disp_in, D.at[pl.ds(0, SEC)]), (scls_in, scls), (lens_in, lens), (stab_in, stab),
        ))
    ]
    for copy in loads:
        copy.start()
    barrier = pltpu.get_barrier_semaphore()

    def greet(p):
        pl.semaphore_signal(barrier, inc=1, device_id={"tile": p}, device_id_type=MESH)

    each_peer(greet)
    for other in (up_g, down_g):
        pl.semaphore_signal(barrier, inc=1, device_id={"stack": other}, device_id_type=MESH)

    def send_rows(par):
        def one(p):
            pltpu.make_async_remote_copy(
                src_ref=msg.at[p], dst_ref=box.at[par, t], send_sem=a_send, recv_sem=a_recv.at[par],
                device_id={"tile": p}, device_id_type=MESH,
            ).start()

        each_peer(one)
        box[par, t] = msg[t]

    def wait_rows(par):
        got = box.at[par, pl.ds(0, TILES - 1)]
        pltpu.make_async_copy(got, got, a_recv.at[par]).wait()
        sent = msg.at[pl.ds(0, TILES - 1)]
        pltpu.make_async_copy(sent, sent, a_send).wait()

    def y_copy(src, dst, sems, recv, index, other):
        return pltpu.make_async_remote_copy(
            src_ref=src, dst_ref=dst, send_sem=sems.at[index], recv_sem=recv.at[index],
            device_id={"stack": other}, device_id_type=MESH,
        )

    def t_copy(src, dst, send, recv, other):
        return pltpu.make_async_remote_copy(
            src_ref=src, dst_ref=dst, send_sem=send, recv_sem=recv,
            device_id={"tile": other}, device_id_type=MESH,
        )

    lane8 = iota((8, 128), 1)
    sub8 = iota((8, 128), 0)
    group8 = lax.shift_right_logical(lane8, 3) - GROW // 8
    own_group = group8 == sub8

    for copy in loads[0:5]:
        copy.wait()
    own = mown[...]
    tri_r, tri_c = iota((128, 256), 0), iota((128, 256), 1)
    tri = jnp.where(tri_r <= tri_c, 1.0, 0.0).astype(BF16)
    lane_own = iota((TILES, 128), 0)
    before = jnp.zeros((TILES, 128), F32)
    src, dst, lev = msrc[...], mdst[...], mlev[...]
    srow, scol = lax.shift_right_logical(src, 7), src & 127
    drow, dcol = lax.shift_right_logical(dst, 7), dst & 127
    live = jnp.where(srow + g * 64 >= STACKS * 64 - 8, 0, lev)
    ints = [v.astype(F32) for v in (srow, scol, drow, dcol, live)]
    slots = jnp.zeros((11 * 16, 128), F32)
    for j in range(8):
        own_j = own[j : j + 1]
        hot = jnp.where(lane_own == own_j, 1.0, 0.0)
        counted = jnp.dot(hot.astype(BF16), tri, preferred_element_type=F32)
        rank = jnp.sum(hot * (counted[:, :128] + before), axis=0, keepdims=True) - 1.0
        before = before + counted[:, 128:]
        rank = rank.astype(I32)
        high = jnp.where(rank >= HALF, 1, 0)
        row_hot = iota((16, 128), 0) == rank - HALF * high
        slot_hot = jnp.where(iota((128, 128), 0) == own_j + TILES * high, 1.0, 0.0).astype(BF16)
        values = [v[j : j + 1] for v in ints]
        for comp in range(2):
            off = moff[comp : comp + 1, j * 128 : (j + 1) * 128]
            first, rest = split(off)
            second, third = split(rest)
            values += [first, second, third]
        picked = jnp.concatenate([jnp.where(row_hot, v, 0.0) for v in values], axis=0).astype(BF16)
        slots = slots + lax.dot_general(picked, slot_hot, (((1,), (1,)), ((), ())), preferred_element_type=F32)
    sl = [slots[16 * v : 16 * v + 16] for v in range(11)]
    mine = sl[0:5] + [sl[5] + sl[6] + sl[7], sl[8] + sl[9] + sl[10]]

    tin[...] = jnp.zeros_like(tin)
    tin[0:112] = jnp.concatenate(mine, axis=0)
    turned = tin[...].T
    msg[:, 0, :] = turned[0:TILES]
    msg[:, 1, :] = turned[TILES:]

    pl.semaphore_wait(barrier, TILES - 1 + 2)
    send_rows(0)

    for copy in loads[5:]:
        copy.wait()
    cls = scls[...]
    stiff = jnp.zeros(cls.shape, F32)
    for k in range(4):
        stiff = jnp.where(cls == k, stab[k], stiff)
    K[0:SEC] = stiff
    C[...] = jnp.zeros_like(C)
    tmp[...] = jnp.zeros_like(tmp)
    for comp in range(2):
        tmp[:, 0:LENS] = lens[:, comp, :]
        wide = fold(tmp[...])
        C[comp : comp + 1] = jnp.sum(jnp.where(own_group, wide, 0.0), axis=0, keepdims=True)

    first = [
        y_copy(D.at[0], D.at[SEC], s_send, s_recv, 0, down_g),
        y_copy(K.at[0], K.at[SEC], s_send, s_recv, 1, down_g),
        y_copy(C, cy, s_send, s_recv, 2, down_g),
    ]
    for copy in first:
        copy.start()

    peer_row = (iota((16, 128), 1) & (TILES - 1)) * 8
    own_row0 = t * 8

    def node_tables(side, values):
        sr, sc, dr, dc = [v.astype(I32) for v in values[0:4]]
        sec = lax.shift_right_logical(sr, 3)
        own_row = sr if side == 0 else sec * 8 + 8 + dr
        own_col = sc if side == 0 else dc
        rowix[side] = own_row
        at = slice(24 * side, 24 * side + 24)
        for n, v in enumerate((own_row, own_col, sec, sc, dc)):
            slotix[n, at] = pack_rows(v, v)
        for i in range(HALF):
            at = slice(i * 128, (i + 1) * 128)
            CH[side, :, at] = jnp.where(iota((128, 128), 0) == own_col[i : i + 1], 1.0, 0.0).astype(BF16)

    def pull_tables(side, values):
        sr, dr = values[0].astype(I32), values[2].astype(I32)
        ox, oy = values[5], values[6]
        sign = 1.0 if side == 0 else -1.0
        s_in = sr & 7
        ysrc = (own_row0 if side == 0 else peer_row) + s_in
        ydst = (peer_row if side == 0 else own_row0) + dr
        ramp_s = (1.0 + ysrc.astype(F32) * (2.0 / 512)) * sign
        ramp_d = (1.0 + ydst.astype(F32) * (2.0 / 512)) * -sign
        weight = values[4] * 0.125
        at = slice(24 * side, 24 * side + 24)
        offs[at] = pack_rows(ox, oy) * sign
        base[at] = pack_rows(weight, weight)
        ramps[0, at] = pack_rows(ramp_s, ramp_s)
        ramps[1, at] = pack_rows(ramp_d, ramp_d)

    def gather(side, first, count):
        d_hi, d_lo = split(D[first : first + count].reshape(count * 16, 128))
        both = jnp.concatenate([d_hi, d_lo], axis=1).astype(BF16)
        for n in range(HALF // 2):
            hot = CH[side, :, n * 256 : (n + 1) * 256]
            got = jnp.dot(both, jnp.concatenate([hot, hot], axis=0), preferred_element_type=F32)
            for m in range(2):
                i = 2 * n + m
                row = rowix[side, i : i + 1]
                sec, within = lax.shift_right_logical(row, 3), row & 7
                at = slice(m * 128, (m + 1) * 128)
                total = [jnp.zeros((8, 128), F32), jnp.zeros((8, 128), F32)]
                for s in range(count):
                    hit = sec == s + first
                    for comp in range(2):
                        r = (s * 2 + comp) * 8
                        total[comp] = jnp.where(hit, got[r : r + 8, at], total[comp])
                for comp in range(2):
                    value = jnp.sum(jnp.where(sub8 == within, total[comp], 0.0), axis=0, keepdims=True)
                    r = rowpos(side, comp, i)
                    tin[r : r + 1] = value

    def by_comp(rows):
        wide = [jnp.broadcast_to(row, (8, 128)) for row in rows]
        return wide + [jnp.where(sub8 < 4, wide[0], wide[1])]

    def gather_edge(side):
        edge = side * SEC
        blocks = [slice(24 * side + 8 * q, 24 * side + 8 * q + 8) for q in range(3)]
        total = [jnp.zeros((8, 128), F32)] * 3
        for r in range(8):
            for q, source in enumerate(by_comp([D[edge, comp, r : r + 1] for comp in range(2)])):
                found = along_lanes(source, slotix[1, blocks[q]])
                total[q] = jnp.where(slotix[0, blocks[q]] == edge * 8 + r, found, total[q])
        for q in range(3):
            tin[blocks[q]] = tin[blocks[q]] + total[q]

    def exchange(par):
        turned = tin[...].T
        for comp in range(2):
            msg[:, comp, :] = turned[comp * TILES : (comp + 1) * TILES] + G[comp : comp + 1]
        send_rows(par)

    node_tables(0, mine)
    tin[...] = jnp.zeros_like(tin)
    gather(0, 0, SEC)
    pull_tables(0, mine)
    for n in range(2):
        k = (iota((128, 128), 1 - n) - GROW) & 7
        turn = (iota((128, 128), n) * k) & 255
        high, low = split(jnp.cos(turn.astype(F32) * (np.pi / 128)))
        COS[n] = jnp.concatenate([high, high, low], axis=0).astype(BF16)
    group16 = lax.shift_right_logical(iota((16, 128), 1), 3) - GROW // 8
    mask16 = (group16 == iota((16, 128), 0)) & (group16 < EXT)

    for copy in first:
        copy.wait()
    for comp in range(2):
        C[comp : comp + 1] = C[comp : comp + 1] + jnp.where(
            group8[0:1] == SEC, pltpu.roll(cy[comp : comp + 1], LENS * SEC, 1), 0.0
        )
    hs[...] = jnp.zeros_like(hs)
    khs[...] = jnp.zeros_like(khs)

    def beside(par):
        return [
            t_copy(hs.at[par, 0], hr.at[par, 1], h_send.at[par, 0], h_recv.at[par, 1], down_t),
            t_copy(hs.at[par, 1], hr.at[par, 0], h_send.at[par, 1], h_recv.at[par, 0], up_t),
        ]

    def send_beside(par):
        for s in range(EXT):
            for comp in range(2):
                r = s * 2 + comp
                hs[par, 0, r : r + 1] = D[s, comp, 0:1]
                hs[par, 1, r : r + 1] = D[s, comp, 7:8]
        for copy in beside(par):
            copy.start()

    for s in range(EXT):
        khs[0, s : s + 1] = K[s, 0:1]
        khs[1, s : s + 1] = K[s, 7:8]
    kcopies = [
        t_copy(khs.at[0], khr.at[1], k_send.at[0], k_recv.at[1], down_t),
        t_copy(khs.at[1], khr.at[0], k_send.at[1], k_recv.at[0], up_t),
    ]
    for copy in kcopies:
        copy.start()
    send_beside(0)

    def shifted(v, low, high):
        above = jnp.where(sub8 == 0, low, pltpu.roll(v, 1, 0))
        below = jnp.where(sub8 == 7, high, pltpu.roll(v, 7, 0))
        for dr, row in ((-1, above), (0, v), (1, below)):
            for dc in (-1, 0, 1):
                if dr or dc:
                    yield row if dc == 0 else pltpu.roll(row, 1 if dc < 0 else 127, 1)

    def turn_rows(par):
        both = jnp.concatenate([box[par, :, 0, :], box[par, :, 1, :]], axis=0)
        return both, both.T

    wait_rows(0)
    _, theirs = turn_rows(0)
    yours = [theirs[16 * v : 16 * v + 16] for v in range(7)]
    node_tables(1, yours)
    gather(1, 1, SEC)
    G[...] = jnp.zeros_like(G)
    exchange(1)
    pull_tables(1, yours)
    for copy in kcopies:
        copy.wait()
    has_low, has_high = jnp.where(t > 0, 1.0, 0.0), jnp.where(t < TILES - 1, 1.0, 0.0)
    for s in range(EXT):
        v = K[s]
        total = jnp.zeros((8, 128), F32)
        near = shifted(v, khr[0, s : s + 1] * has_low, khr[1, s : s + 1] * has_high)
        for n, ((dr, dc, scale), other) in enumerate(zip(STEPS, near)):
            w = scale * jnp.minimum(v, other)
            if dc:
                w = jnp.where(lane8 == (0 if dc < 0 else 127), 0.0, w)
            W[n, s] = w
            total = total + w
        WS[s] = total

    wrow[...] = jnp.zeros_like(wrow)

    ramp8 = 1.0 + (own_row0 + sub8).astype(F32) * (2.0 / 512)
    lens_step = LENS_RATE * SEC / (1024 * TILES)

    def take_gradient(both):
        for comp in range(2):
            total = jnp.sum(both[comp * TILES : (comp + 1) * TILES], axis=0, keepdims=True)
            C[comp : comp + 1] = C[comp : comp + 1] + lens_step * jnp.where(group8[0:1] >= 0, total, 0.0)

    def lens_values():
        rows = []
        for comp in range(2):
            wide = jnp.broadcast_to(C[comp : comp + 1], (16, 128))
            rows.append(jnp.where(mask16, wide, 0.0))
        c_hi, c_lo = split(jnp.concatenate(rows, axis=0))
        cat = jnp.concatenate([c_hi, c_lo, c_hi], axis=1).astype(BF16)
        L[...] = jnp.dot(cat, COS[1], preferred_element_type=F32).reshape(2, 16, 128)
        sources = [by_comp([L[comp, s : s + 1] for comp in range(2)]) for s in range(EXT)]
        for b in range(6):
            at = slice(8 * b, 8 * b + 8)
            q = b % 3
            sec = slotix[2, at]
            own_end, far_end = jnp.zeros((8, 128), F32), jnp.zeros((8, 128), F32)
            for s in range(SEC):
                hit = sec == s
                own_end = jnp.where(hit, along_lanes(sources[s][q], slotix[3, at]), own_end)
                far_end = jnp.where(hit, along_lanes(sources[s + 1][q], slotix[4, at]), far_end)
            lval[at] = ramps[0, at] * own_end + ramps[1, at] * far_end

    def forces(theirs):
        other = jnp.concatenate([theirs[24:48], theirs[0:24]], axis=0)
        r = tin[0:48] - other + offs[...] + lval[...]
        sq = r * r
        for side in range(2):
            b = side * 24
            near = sq[b : b + 8] + sq[b + 8 : b + 16]
            last = sq[b + 16 : b + 24]
            last = last + pltpu.roll(last, 4, 0)
            size = jnp.concatenate([near, near, last], axis=0)
            pull[b : b + 24] = -base[b : b + 24] * r[b : b + 24] / (1.0 + size * 0.25)

    def scatter(side, first, count):
        rows = iota((count * 8, 128), 0) + first * 8
        total = jnp.zeros((4 * count * 8, 128), F32)
        for n in range(HALF // 2):
            cols = []
            for m in range(2):
                i = 2 * n + m
                hit = rows == rowix[side, i : i + 1]
                pieces = []
                for comp in range(2):
                    r = rowpos(side, comp, i)
                    pieces += list(split(pull[r : r + 1]))
                cols.append(jnp.concatenate([jnp.where(hit, p, 0.0) for p in pieces], axis=0))
            spread = jnp.concatenate(cols, axis=1).astype(BF16)
            total = total + lax.dot_general(
                spread, CH[side, :, n * 256 : (n + 1) * 256], (((1,), (1,)), ((), ())),
                preferred_element_type=F32,
            )
        total = total.reshape(2, 2, count, 8, 128)
        return [total[comp, 0] + total[comp, 1] for comp in range(2)]

    def springs(par):
        for s in range(EXT):
            for comp in range(2):
                r = s * 2 + comp
                v = D[s, comp]
                total = -WS[s] * v
                near = shifted(v, hr[par, 0, r : r + 1], hr[par, 1, r : r + 1])
                for n, other in enumerate(near):
                    total = total + W[n, s] * other
                S[s, comp] = total

    def ramp_sums(sections):
        for s in sections:
            for comp in range(2):
                r = comp * 16 + s
                wrow[r : r + 1] = jnp.sum(ramp8 * F[s, comp], axis=0, keepdims=True)

    def gradient():
        w_hi, w_lo = split(wrow[...])
        cat = jnp.concatenate([w_hi, w_lo, w_hi], axis=1).astype(BF16)
        out = jnp.dot(cat, COS[0], preferred_element_type=F32)
        for comp in range(2):
            G[comp : comp + 1] = jnp.sum(
                jnp.where(mask16, out[comp * 16 : comp * 16 + 16], 0.0), axis=0, keepdims=True
            )

    def arrive(it):
        par = lax.rem(it + 1, 2)
        hpar = lax.rem(it, 2)
        for copy in beside(hpar):
            copy.wait()
        springs(hpar)
        wait_rows(par)
        both, theirs = turn_rows(par)
        take_gradient(both)
        lens_values()
        forces(theirs)
        for side, edge in ((1, SEC), (0, 0)):
            on_edge = scatter(side, edge, 1)
            for comp in range(2):
                F[edge, comp] = on_edge[comp][0]
            ys[hpar, 1 - side] = F[edge]
        copies = [y_pair(hpar, 0, up_g), y_pair(hpar, 1, down_g)]
        for copy in copies:
            copy.start()
        return par, hpar, copies

    def inner_forces():
        inner = [scatter(side, 1, SEC - 1) for side in range(2)]
        for comp in range(2):
            F[1:SEC, comp] = inner[0][comp] + inner[1][comp]
        ramp_sums(range(1, SEC))

    def sweep(it, carry):
        par, hpar, copies = arrive(it)
        inner_forces()
        D[1:SEC] = D[1:SEC] + STEP_RATE * (S[1:SEC] + F[1:SEC])
        gather(0, 1, SEC - 1)
        gather(1, 1, SEC - 1)
        for copy in copies:
            copy.wait()
        for way, edge in ((0, 0), (1, SEC)):
            F[edge] = F[edge] + yr[hpar, way]
            D[edge] = D[edge] + STEP_RATE * (S[edge] + F[edge])
        ramp_sums((0, SEC))
        gradient()

        gather_edge(0)
        gather_edge(1)
        exchange(1 - par)
        send_beside(1 - hpar)
        return carry

    def y_pair(par, way, other):
        return pltpu.make_async_remote_copy(
            src_ref=ys.at[par, way], dst_ref=yr.at[par, way], send_sem=y_send.at[par, way],
            recv_sem=y_recv.at[par, way], device_id={"stack": other}, device_id_type=MESH,
        )

    lax.fori_loop(0, ITERS - 1, sweep, 0)

    last, lpar, copies = arrive(ITERS - 1)
    inner_forces()
    ramp_sums((0, SEC))
    gradient()
    gmsg[...] = G[0:2]
    fin = 1 - last

    def send_gradient(p):
        pltpu.make_async_remote_copy(
            src_ref=gmsg, dst_ref=box.at[fin, t], send_sem=a_send, recv_sem=a_recv.at[fin],
            device_id={"tile": p}, device_id_type=MESH,
        ).start()

    def send_edge(p):
        pltpu.make_async_remote_copy(
            src_ref=gmsg, dst_ref=ebox.at[t], send_sem=e_send, recv_sem=e_recv,
            device_id={"stack": up_g, "tile": p}, device_id_type=MESH,
        ).start()

    def send_both(p):
        send_edge(p)
        send_gradient(p)

    each_peer(send_both)
    send_edge(t)
    box[fin, t] = gmsg[...]
    for copy in copies:
        copy.wait()
    F[0] = F[0] + yr[lpar, 0]
    dout[...] = D[0:SEC] + STEP_RATE * (S[0:SEC] + F[0:SEC])
    wait_rows(fin)
    pltpu.make_async_copy(ebox, ebox, e_recv).wait()
    pltpu.make_async_copy(ebox, ebox, e_send).wait()
    for comp in range(2):
        total = jnp.sum(box[fin, :, comp, :], axis=0, keepdims=True)
        below = jnp.sum(ebox[:, comp, :], axis=0, keepdims=True)
        below = pltpu.roll(below, 128 - LENS * SEC, 1)
        first = jnp.where(group8[0:1] == 0, below, 0.0)
        total = jnp.where((group8[0:1] >= 0) & (group8[0:1] < SEC), total + first, 0.0)
        C[comp : comp + 1] = C[comp : comp + 1] + lens_step * total
    for comp in range(2):
        wide = fold(jnp.where(own_group, jnp.broadcast_to(C[comp : comp + 1], (8, 128)), 0.0))
        cout[:, comp, :] = wide[:, 0:LENS]


def on_device(displacement, lens_coef, stiff_class, stiff_table, match_src, match_owner, match_dst, match_level, match_offset):
    vmem = pl.BlockSpec(memory_space=pltpu.VMEM)
    hbm = pl.BlockSpec(memory_space=pltpu.HBM)
    V, DMA = pltpu.VMEM, pltpu.SemaphoreType.DMA
    lists = [a.reshape(8, 128) for a in (match_src, match_owner, match_dst, match_level)]
    scratch = [
        V((SEC, 2, LENS), F32),
        V((SEC, 8, 128), I32),
        pltpu.SMEM((4,), F32),
        V((8, 128), I32), V((8, 128), I32), V((8, 128), I32), V((8, 128), I32),
        V((2, 1024), F32),
        V((EXT, 2, 8, 128), F32),
        V((EXT, 8, 128), F32),
        V((8, EXT, 8, 128), F32),
        V((EXT, 8, 128), F32),
        V((EXT, 2, 8, 128), F32),
        V((EXT, 2, 8, 128), F32),
        V((TILES, 2, 128), F32),
        V((2, TILES, 2, 128), F32),
        V((2, 128), F32),
        V((TILES, 2, 128), F32),
        V((2, 128, HALF * 128), BF16),
        V((2, 3 * 128, 128), BF16),
        V((2, 16, 128), F32),
        V((2, 16, 128), I32),
        V((5, 48, 128), I32),
        V((2, 48, 128), F32),
        V((48, 128), F32),
        V((48, 128), F32),
        V((128, 128), F32),
        V((48, 128), F32),
        V((48, 128), F32),
        V((8, 128), F32),
        V((8, 128), F32),
        V((8, 128), F32),
        V((32, 128), F32),
        V((2, 2, 24, 128), F32),
        V((2, 2, 24, 128), F32),
        V((2, 16, 128), F32),
        V((2, 16, 128), F32),
        V((2, 2, 2, 8, 128), F32),
        V((2, 2, 2, 8, 128), F32),
        V((8, 128), F32),
        DMA((9,)), DMA, DMA((2,)), DMA((2, 2)), DMA((2, 2)), DMA((2,)), DMA((2,)), DMA((2, 2)), DMA((2, 2)), DMA((3,)), DMA((3,)), DMA, DMA,
    ]
    outs = (
        jax.ShapeDtypeStruct((SEC, 2, 8, 128), F32),
        jax.ShapeDtypeStruct((SEC, 2, LENS), F32),
    )
    return pl.pallas_call(
        kernel,
        out_shape=outs,
        in_specs=[hbm] * 9,
        out_specs=(vmem, vmem),
        scratch_shapes=scratch,
        compiler_params=pltpu.CompilerParams(
            collective_id=0, has_side_effects=True
        ),
        name="relax",
    )(displacement, lens_coef, stiff_class, stiff_table, *lists, match_offset)


def solution(mesh):
    in_specs = (
        P("stack", None, "tile", None),
        P("stack", None, None),
        P("stack", "tile", None),
        P(),
        P(("stack", "tile")),
        P(("stack", "tile"), None),
        P(("stack", "tile")),
        P(("stack", "tile")),
        P(None, ("stack", "tile")),
    )
    out_specs = (P("stack", None, "tile", None), P("stack", None, None))
    return jax.shard_map(on_device, mesh=mesh, in_specs=in_specs, out_specs=out_specs, check_vma=False)
```

```python
import functools

import jax
import jax.numpy as jnp
import numpy as np
from jax import lax
from jax.experimental import pallas as pl
from jax.experimental.pallas import tpu as pltpu
from jax.sharding import PartitionSpec as P

ITERS = 4
STEP_RATE = 0.04
LENS_RATE = 4.0
MESH = pl.DeviceIdType.MESH
F32, BF16, I32 = jnp.float32, jnp.bfloat16, jnp.int32

SEC, EXT = 8, 9
TILES, STACKS = 64, 4
HALF = 12
GROW = 48
LENS = 8

NEAR = [(dx, dc) for dx in (2, 1, 3, 0) for dc in (1, 0)]
STEPS = [(dr, dc, 1.0 if dr == 0 or dc == 0 else 0.5) for dr in (-1, 0, 1) for dc in (-1, 0, 1) if dr or dc]


def iota(shape, dim):
    return lax.broadcasted_iota(I32, shape, dim)


def split(x):
    high = x.astype(BF16).astype(F32)
    return high, x - high


def rowpos(side, comp, i):
    return side * 24 + (comp * 8 + i if i < 8 else 16 + comp * 4 + i - 8)


def fold(x):
    for step in (8, 16, 32, 64):
        x = x + pltpu.roll(x, step, 1)
    return x


def along_lanes(source, lanes):
    dims = lax.GatherDimensionNumbers(
        offset_dims=(), collapsed_slice_dims=(1,), start_index_map=(1,),
        operand_batching_dims=(0,), start_indices_batching_dims=(0,),
    )
    return lax.gather(
        source, lanes[:, :, None], dims, slice_sizes=(1, 1), mode=lax.GatherScatterMode.PROMISE_IN_BOUNDS
    )


def pack_rows(a, b):
    last = jnp.where(iota((8, 128), 0) < 4, a[8:16], pltpu.roll(b[8:16], 4, 0))
    return jnp.concatenate([a[0:8], b[0:8], last], axis=0)


def kernel(
    disp_in, lens_in, scls_in, stab_in, msrc_in, mown_in, mdst_in, mlev_in, moff_in,
    dout, cout,
    lens, scls, stab, msrc, mown, mdst, mlev, moff,
    D, K, W, WS, S, F, msg, box, gmsg, ebox, CH, CHT, COS, L, rowix, slotix, ramps, offs, base, tin, pull, lval, C, G, tmp, wrow,
    hs, hr, khs, khr, ys, yr, cy,
    in_sem, a_send, a_recv, h_send, h_recv, k_send, k_recv, y_send, y_recv, s_send, s_recv, e_send, e_recv,
):
    t = lax.axis_index("tile")
    g = lax.axis_index("stack")
    z, a = lax.div(t, 8), lax.rem(t, 8)
    x, c = lax.div(a, 2), lax.rem(a, 2)
    up_g, down_g = lax.rem(g + 1, STACKS), lax.rem(g + STACKS - 1, STACKS)
    up_t, down_t = lax.rem(t + 1, TILES), lax.rem(t + TILES - 1, TILES)

    def peer(dz, dx, dc):
        pz, px, pc = lax.rem(z + dz, 8), lax.rem(x + dx, 4), lax.rem(c + dc, 2)
        return pz * 8 + px * 2 + pc

    def each_peer(do):
        def along_z(k, carry):
            odd = lax.rem(k, 2)
            dz = 4 + lax.div(k, 2) - odd * (k)
            for dx, dc in NEAR:
                do(peer(dz, dx, dc))
            return carry

        lax.fori_loop(0, 7, along_z, 0)
        for dx, dc in NEAR:
            if dx or dc:
                do(peer(0, dx, dc))

    loads = [
        pltpu.make_async_copy(src, dst, in_sem.at[n])
        for n, (src, dst) in enumerate((
            (mown_in, mown), (msrc_in, msrc), (mdst_in, mdst), (mlev_in, mlev), (moff_in, moff),
            (disp_in, D.at[pl.ds(0, SEC)]), (scls_in, scls), (lens_in, lens), (stab_in, stab),
        ))
    ]
    for copy in loads:
        copy.start()
    barrier = pltpu.get_barrier_semaphore()

    def greet(p):
        pl.semaphore_signal(barrier, inc=1, device_id={"tile": p}, device_id_type=MESH)

    each_peer(greet)
    for other in (up_g, down_g):
        pl.semaphore_signal(barrier, inc=1, device_id={"stack": other}, device_id_type=MESH)

    def send_rows(par):
        def one(p):
            pltpu.make_async_remote_copy(
                src_ref=msg.at[p], dst_ref=box.at[par, t], send_sem=a_send, recv_sem=a_recv.at[par],
                device_id={"tile": p}, device_id_type=MESH,
            ).start()

        each_peer(one)
        box[par, t] = msg[t]

    def wait_rows(par):
        got = box.at[par, pl.ds(0, TILES - 1)]
        pltpu.make_async_copy(got, got, a_recv.at[par]).wait()
        sent = msg.at[pl.ds(0, TILES - 1)]
        pltpu.make_async_copy(sent, sent, a_send).wait()

    def y_copy(src, dst, sems, recv, index, other):
        return pltpu.make_async_remote_copy(
            src_ref=src, dst_ref=dst, send_sem=sems.at[index], recv_sem=recv.at[index],
            device_id={"stack": other}, device_id_type=MESH,
        )

    def t_copy(src, dst, send, recv, other):
        return pltpu.make_async_remote_copy(
            src_ref=src, dst_ref=dst, send_sem=send, recv_sem=recv,
            device_id={"tile": other}, device_id_type=MESH,
        )

    lane8 = iota((8, 128), 1)
    sub8 = iota((8, 128), 0)
    group8 = lax.shift_right_logical(lane8, 3) - GROW // 8
    own_group = group8 == sub8

    for copy in loads[0:5]:
        copy.wait()
    own = mown[...]
    tri_r, tri_c = iota((128, 256), 0), iota((128, 256), 1)
    tri = jnp.where(tri_r <= tri_c, 1.0, 0.0).astype(BF16)
    lane_own = iota((TILES, 128), 0)
    before = jnp.zeros((TILES, 128), F32)
    src, dst, lev = msrc[...], mdst[...], mlev[...]
    srow, scol = lax.shift_right_logical(src, 7), src & 127
    drow, dcol = lax.shift_right_logical(dst, 7), dst & 127
    live = jnp.where(srow + g * 64 >= STACKS * 64 - 8, 0, lev)
    ints = [v.astype(F32) for v in (srow, scol, drow, dcol, live)]
    slots = jnp.zeros((11 * 16, 128), F32)
    for j in range(8):
        own_j = own[j : j + 1]
        hot = jnp.where(lane_own == own_j, 1.0, 0.0)
        counted = jnp.dot(hot.astype(BF16), tri, preferred_element_type=F32)
        rank = jnp.sum(hot * (counted[:, :128] + before), axis=0, keepdims=True) - 1.0
        before = before + counted[:, 128:]
        rank = rank.astype(I32)
        high = jnp.where(rank >= HALF, 1, 0)
        row_hot = iota((16, 128), 0) == rank - HALF * high
        slot_hot = jnp.where(iota((128, 128), 0) == own_j + TILES * high, 1.0, 0.0).astype(BF16)
        values = [v[j : j + 1] for v in ints]
        for comp in range(2):
            off = moff[comp : comp + 1, j * 128 : (j + 1) * 128]
            first, rest = split(off)
            second, third = split(rest)
            values += [first, second, third]
        picked = jnp.concatenate([jnp.where(row_hot, v, 0.0) for v in values], axis=0).astype(BF16)
        slots = slots + lax.dot_general(picked, slot_hot, (((1,), (1,)), ((), ())), preferred_element_type=F32)
    sl = [slots[16 * v : 16 * v + 16] for v in range(11)]
    mine = sl[0:5] + [sl[5] + sl[6] + sl[7], sl[8] + sl[9] + sl[10]]

    tin[...] = jnp.zeros_like(tin)
    tin[0:112] = jnp.concatenate(mine, axis=0)
    turned = tin[...].T
    msg[:, 0, :] = turned[0:TILES]
    msg[:, 1, :] = turned[TILES:]

    pl.semaphore_wait(barrier, TILES - 1 + 2)
    send_rows(0)

    for copy in loads[5:]:
        copy.wait()
    cls = scls[...]
    stiff = jnp.zeros(cls.shape, F32)
    for k in range(4):
        stiff = jnp.where(cls == k, stab[k], stiff)
    K[0:SEC] = stiff
    C[...] = jnp.zeros_like(C)
    tmp[...] = jnp.zeros_like(tmp)
    for comp in range(2):
        tmp[:, 0:LENS] = lens[:, comp, :]
        wide = fold(tmp[...])
        C[comp : comp + 1] = jnp.sum(jnp.where(own_group, wide, 0.0), axis=0, keepdims=True)

    first = [
        y_copy(D.at[0], D.at[SEC], s_send, s_recv, 0, down_g),
        y_copy(K.at[0], K.at[SEC], s_send, s_recv, 1, down_g),
        y_copy(C, cy, s_send, s_recv, 2, down_g),
    ]
    for copy in first:
        copy.start()

    peer_row = (iota((16, 128), 1) & (TILES - 1)) * 8
    own_row0 = t * 8

    def node_tables(side, values):
        sr, sc, dr, dc = [v.astype(I32) for v in values[0:4]]
        sec = lax.shift_right_logical(sr, 3)
        own_row = sr if side == 0 else sec * 8 + 8 + dr
        own_col = sc if side == 0 else dc
        rowix[side] = own_row
        at = slice(24 * side, 24 * side + 24)
        for n, v in enumerate((own_row, own_col, sec, sc, dc)):
            slotix[n, at] = pack_rows(v, v)
        for i in range(HALF):
            at = slice(i * 128, (i + 1) * 128)
            CH[side, :, at] = jnp.where(iota((128, 128), 0) == own_col[i : i + 1], 1.0, 0.0).astype(BF16)

    def pull_tables(side, values):
        sr, dr = values[0].astype(I32), values[2].astype(I32)
        ox, oy = values[5], values[6]
        sign = 1.0 if side == 0 else -1.0
        s_in = sr & 7
        ysrc = (own_row0 if side == 0 else peer_row) + s_in
        ydst = (peer_row if side == 0 else own_row0) + dr
        ramp_s = (1.0 + ysrc.astype(F32) * (2.0 / 512)) * sign
        ramp_d = (1.0 + ydst.astype(F32) * (2.0 / 512)) * -sign
        weight = values[4] * 0.125
        at = slice(24 * side, 24 * side + 24)
        offs[at] = pack_rows(ox, oy) * sign
        base[at] = pack_rows(weight, weight)
        ramps[0, at] = pack_rows(ramp_s, ramp_s)
        ramps[1, at] = pack_rows(ramp_d, ramp_d)
        own_col = (values[1] if side == 0 else values[3]).astype(I32)
        for i in range(HALF):
            hot = jnp.where(iota((128, 128), 0) == own_col[i : i + 1], 1.0, 0.0)
            CHT[side, i * 128 : (i + 1) * 128] = hot.T.astype(BF16)

    def gather(side, first, count):
        d_hi, d_lo = split(D[first : first + count].reshape(count * 16, 128))
        both = jnp.concatenate([d_hi, d_lo], axis=1).astype(BF16)
        for n in range(HALF // 2):
            hot = CH[side, :, n * 256 : (n + 1) * 256]
            got = jnp.dot(both, jnp.concatenate([hot, hot], axis=0), preferred_element_type=F32)
            for m in range(2):
                i = 2 * n + m
                row = rowix[side, i : i + 1]
                sec, within = lax.shift_right_logical(row, 3), row & 7
                at = slice(m * 128, (m + 1) * 128)
                total = [jnp.zeros((8, 128), F32), jnp.zeros((8, 128), F32)]
                for s in range(count):
                    hit = sec == s + first
                    for comp in range(2):
                        r = (s * 2 + comp) * 8
                        total[comp] = jnp.where(hit, got[r : r + 8, at], total[comp])
                for comp in range(2):
                    value = jnp.sum(jnp.where(sub8 == within, total[comp], 0.0), axis=0, keepdims=True)
                    r = rowpos(side, comp, i)
                    tin[r : r + 1] = value

    def by_comp(rows):
        wide = [jnp.broadcast_to(row, (8, 128)) for row in rows]
        return wide + [jnp.where(sub8 < 4, wide[0], wide[1])]

    def gather_edge(side):
        edge = side * SEC
        blocks = [slice(24 * side + 8 * q, 24 * side + 8 * q + 8) for q in range(3)]
        total = [jnp.zeros((8, 128), F32)] * 3
        for r in range(8):
            for q, source in enumerate(by_comp([D[edge, comp, r : r + 1] for comp in range(2)])):
                found = along_lanes(source, slotix[1, blocks[q]])
                total[q] = jnp.where(slotix[0, blocks[q]] == edge * 8 + r, found, total[q])
        for q in range(3):
            tin[blocks[q]] = tin[blocks[q]] + total[q]

    def exchange(par):
        turned = tin[...].T
        flat = msg.reshape(128, 128)
        for comp in range(2):
            flat[pl.ds(comp, TILES, stride=2), :] = turned[comp * TILES : (comp + 1) * TILES] + G[comp : comp + 1]
        send_rows(par)

    node_tables(0, mine)
    tin[...] = jnp.zeros_like(tin)
    gather(0, 0, SEC)
    pull_tables(0, mine)
    for n in range(2):
        k = (iota((128, 128), 1 - n) - GROW) & 7
        turn = (iota((128, 128), n) * k) & 255
        high, low = split(jnp.cos(turn.astype(F32) * (np.pi / 128)))
        COS[n] = jnp.concatenate([high, high, low], axis=0).astype(BF16)
    group16 = lax.shift_right_logical(iota((16, 128), 1), 3) - GROW // 8
    mask16 = (group16 == iota((16, 128), 0)) & (group16 < EXT)

    for copy in first:
        copy.wait()
    for comp in range(2):
        C[comp : comp + 1] = C[comp : comp + 1] + jnp.where(
            group8[0:1] == SEC, pltpu.roll(cy[comp : comp + 1], LENS * SEC, 1), 0.0
        )
    hs[...] = jnp.zeros_like(hs)
    khs[...] = jnp.zeros_like(khs)

    def beside(par):
        return [
            t_copy(hs.at[par, 0], hr.at[par, 1], h_send.at[par, 0], h_recv.at[par, 1], down_t),
            t_copy(hs.at[par, 1], hr.at[par, 0], h_send.at[par, 1], h_recv.at[par, 0], up_t),
        ]

    def send_beside(par):
        for s in range(EXT):
            for comp in range(2):
                r = s * 2 + comp
                hs[par, 0, r : r + 1] = D[s, comp, 0:1]
                hs[par, 1, r : r + 1] = D[s, comp, 7:8]
        for copy in beside(par):
            copy.start()

    for s in range(EXT):
        khs[0, s : s + 1] = K[s, 0:1]
        khs[1, s : s + 1] = K[s, 7:8]
    kcopies = [
        t_copy(khs.at[0], khr.at[1], k_send.at[0], k_recv.at[1], down_t),
        t_copy(khs.at[1], khr.at[0], k_send.at[1], k_recv.at[0], up_t),
    ]
    for copy in kcopies:
        copy.start()
    send_beside(0)

    def shifted(v, low, high):
        above = jnp.where(sub8 == 0, low, pltpu.roll(v, 1, 0))
        below = jnp.where(sub8 == 7, high, pltpu.roll(v, 7, 0))
        for dr, row in ((-1, above), (0, v), (1, below)):
            for dc in (-1, 0, 1):
                if dr or dc:
                    yield row if dc == 0 else pltpu.roll(row, 1 if dc < 0 else 127, 1)

    def turn_rows(par):
        flat = box.at[par].reshape(128, 128)
        both = jnp.concatenate([flat[pl.ds(n, TILES, stride=2), :] for n in range(2)], axis=0)
        return both, both.T

    wait_rows(0)
    _, theirs = turn_rows(0)
    yours = [theirs[16 * v : 16 * v + 16] for v in range(7)]
    node_tables(1, yours)
    gather(1, 1, SEC)
    G[...] = jnp.zeros_like(G)
    exchange(1)
    pull_tables(1, yours)
    for copy in kcopies:
        copy.wait()
    has_low, has_high = jnp.where(t > 0, 1.0, 0.0), jnp.where(t < TILES - 1, 1.0, 0.0)
    for s in range(EXT):
        v = K[s]
        total = jnp.zeros((8, 128), F32)
        near = shifted(v, khr[0, s : s + 1] * has_low, khr[1, s : s + 1] * has_high)
        for n, ((dr, dc, scale), other) in enumerate(zip(STEPS, near)):
            w = scale * jnp.minimum(v, other)
            if dc:
                w = jnp.where(lane8 == (0 if dc < 0 else 127), 0.0, w)
            W[n, s] = w
            total = total + w
        WS[s] = total

    wrow[...] = jnp.zeros_like(wrow)

    ramp8 = 1.0 + (own_row0 + sub8).astype(F32) * (2.0 / 512)
    lens_step = LENS_RATE * SEC / (1024 * TILES)

    def take_gradient(both):
        for comp in range(2):
            total = jnp.sum(both[comp * TILES : (comp + 1) * TILES], axis=0, keepdims=True)
            C[comp : comp + 1] = C[comp : comp + 1] + lens_step * jnp.where(group8[0:1] >= 0, total, 0.0)

    def lens_values():
        rows = []
        for comp in range(2):
            wide = jnp.broadcast_to(C[comp : comp + 1], (16, 128))
            rows.append(jnp.where(mask16, wide, 0.0))
        c_hi, c_lo = split(jnp.concatenate(rows, axis=0))
        cat = jnp.concatenate([c_hi, c_lo, c_hi], axis=1).astype(BF16)
        L[...] = jnp.dot(cat, COS[1], preferred_element_type=F32).reshape(2, 16, 128)
        sources = [by_comp([L[comp, s : s + 1] for comp in range(2)]) for s in range(EXT)]
        for b in range(6):
            at = slice(8 * b, 8 * b + 8)
            q = b % 3
            sec = slotix[2, at]
            own_end, far_end = jnp.zeros((8, 128), F32), jnp.zeros((8, 128), F32)
            for s in range(SEC):
                hit = sec == s
                own_end = jnp.where(hit, along_lanes(sources[s][q], slotix[3, at]), own_end)
                far_end = jnp.where(hit, along_lanes(sources[s + 1][q], slotix[4, at]), far_end)
            lval[at] = ramps[0, at] * own_end + ramps[1, at] * far_end

    def forces(theirs):
        other = jnp.concatenate([theirs[24:48], theirs[0:24]], axis=0)
        r = tin[0:48] - other + offs[...] + lval[...]
        sq = r * r
        for side in range(2):
            b = side * 24
            near = sq[b : b + 8] + sq[b + 8 : b + 16]
            last = sq[b + 16 : b + 24]
            last = last + pltpu.roll(last, 4, 0)
            size = jnp.concatenate([near, near, last], axis=0)
            pull[b : b + 24] = -base[b : b + 24] * r[b : b + 24] / (1.0 + size * 0.25)

    def scatter(side, first, count):
        rows = iota((count * 8, 128), 0) + first * 8
        total = jnp.zeros((4 * count * 8, 128), F32)
        for n in range(HALF // 2):
            cols = []
            for m in range(2):
                i = 2 * n + m
                hit = rows == rowix[side, i : i + 1]
                pieces = []
                for comp in range(2):
                    r = rowpos(side, comp, i)
                    pieces += list(split(pull[r : r + 1]))
                cols.append(jnp.concatenate([jnp.where(hit, p, 0.0) for p in pieces], axis=0))
            spread = jnp.concatenate(cols, axis=1).astype(BF16)
            total = total + jnp.dot(
                spread, CHT[side, n * 256 : (n + 1) * 256], preferred_element_type=F32
            )
        total = total.reshape(2, 2, count, 8, 128)
        return [total[comp, 0] + total[comp, 1] for comp in range(2)]

    def springs(par):
        for s in range(EXT):
            for comp in range(2):
                r = s * 2 + comp
                v = D[s, comp]
                total = -WS[s] * v
                near = shifted(v, hr[par, 0, r : r + 1], hr[par, 1, r : r + 1])
                for n, other in enumerate(near):
                    total = total + W[n, s] * other
                S[s, comp] = total

    def ramp_sums(sections):
        for s in sections:
            for comp in range(2):
                r = comp * 16 + s
                wrow[r : r + 1] = jnp.sum(ramp8 * F[s, comp], axis=0, keepdims=True)

    def gradient():
        w_hi, w_lo = split(wrow[...])
        cat = jnp.concatenate([w_hi, w_lo, w_hi], axis=1).astype(BF16)
        out = jnp.dot(cat, COS[0], preferred_element_type=F32)
        for comp in range(2):
            G[comp : comp + 1] = jnp.sum(
                jnp.where(mask16, out[comp * 16 : comp * 16 + 16], 0.0), axis=0, keepdims=True
            )

    def arrive(it):
        par = lax.rem(it + 1, 2)
        hpar = lax.rem(it, 2)
        for copy in beside(hpar):
            copy.wait()
        springs(hpar)
        wait_rows(par)
        both, theirs = turn_rows(par)
        take_gradient(both)
        lens_values()
        forces(theirs)
        for side, edge in ((1, SEC), (0, 0)):
            on_edge = scatter(side, edge, 1)
            for comp in range(2):
                F[edge, comp] = on_edge[comp][0]
            ys[hpar, 1 - side] = F[edge]
        copies = [y_pair(hpar, 0, up_g), y_pair(hpar, 1, down_g)]
        for copy in copies:
            copy.start()
        return par, hpar, copies

    def inner_forces():
        inner = [scatter(side, 1, SEC - 1) for side in range(2)]
        for comp in range(2):
            F[1:SEC, comp] = inner[0][comp] + inner[1][comp]
        ramp_sums(range(1, SEC))

    def sweep(it, carry):
        par, hpar, copies = arrive(it)
        inner_forces()
        D[1:SEC] = D[1:SEC] + STEP_RATE * (S[1:SEC] + F[1:SEC])
        gather(0, 1, SEC - 1)
        gather(1, 1, SEC - 1)
        for copy in copies:
            copy.wait()
        for way, edge in ((0, 0), (1, SEC)):
            F[edge] = F[edge] + yr[hpar, way]
            D[edge] = D[edge] + STEP_RATE * (S[edge] + F[edge])
        ramp_sums((0, SEC))
        gradient()

        gather_edge(0)
        gather_edge(1)
        exchange(1 - par)
        send_beside(1 - hpar)
        return carry

    def y_pair(par, way, other):
        return pltpu.make_async_remote_copy(
            src_ref=ys.at[par, way], dst_ref=yr.at[par, way], send_sem=y_send.at[par, way],
            recv_sem=y_recv.at[par, way], device_id={"stack": other}, device_id_type=MESH,
        )

    lax.fori_loop(0, ITERS - 1, sweep, 0)

    last, lpar, copies = arrive(ITERS - 1)
    inner_forces()
    ramp_sums((0, SEC))
    gradient()
    gmsg[...] = G[0:2]
    fin = 1 - last

    def send_gradient(p):
        pltpu.make_async_remote_copy(
            src_ref=gmsg, dst_ref=box.at[fin, t], send_sem=a_send, recv_sem=a_recv.at[fin],
            device_id={"tile": p}, device_id_type=MESH,
        ).start()

    def send_edge(p):
        pltpu.make_async_remote_copy(
            src_ref=gmsg, dst_ref=ebox.at[t], send_sem=e_send, recv_sem=e_recv,
            device_id={"stack": up_g, "tile": p}, device_id_type=MESH,
        ).start()

    def send_both(p):
        send_edge(p)
        send_gradient(p)

    each_peer(send_both)
    send_edge(t)
    box[fin, t] = gmsg[...]
    for copy in copies:
        copy.wait()
    F[0] = F[0] + yr[lpar, 0]
    dout[...] = D[0:SEC] + STEP_RATE * (S[0:SEC] + F[0:SEC])
    wait_rows(fin)
    pltpu.make_async_copy(ebox, ebox, e_recv).wait()
    pltpu.make_async_copy(ebox, ebox, e_send).wait()
    for comp in range(2):
        total = jnp.sum(box[fin, :, comp, :], axis=0, keepdims=True)
        below = jnp.sum(ebox[:, comp, :], axis=0, keepdims=True)
        below = pltpu.roll(below, 128 - LENS * SEC, 1)
        first = jnp.where(group8[0:1] == 0, below, 0.0)
        total = jnp.where((group8[0:1] >= 0) & (group8[0:1] < SEC), total + first, 0.0)
        C[comp : comp + 1] = C[comp : comp + 1] + lens_step * total
    for comp in range(2):
        wide = fold(jnp.where(own_group, jnp.broadcast_to(C[comp : comp + 1], (8, 128)), 0.0))
        cout[:, comp, :] = wide[:, 0:LENS]


def on_device(displacement, lens_coef, stiff_class, stiff_table, match_src, match_owner, match_dst, match_level, match_offset):
    vmem = pl.BlockSpec(memory_space=pltpu.VMEM)
    hbm = pl.BlockSpec(memory_space=pltpu.HBM)
    V, DMA = pltpu.VMEM, pltpu.SemaphoreType.DMA
    lists = [a.reshape(8, 128) for a in (match_src, match_owner, match_dst, match_level)]
    scratch = [
        V((SEC, 2, LENS), F32),
        V((SEC, 8, 128), I32),
        pltpu.SMEM((4,), F32),
        V((8, 128), I32), V((8, 128), I32), V((8, 128), I32), V((8, 128), I32),
        V((2, 1024), F32),
        V((EXT, 2, 8, 128), F32),
        V((EXT, 8, 128), F32),
        V((8, EXT, 8, 128), F32),
        V((EXT, 8, 128), F32),
        V((EXT, 2, 8, 128), F32),
        V((EXT, 2, 8, 128), F32),
        V((TILES, 2, 128), F32),
        V((2, TILES, 2, 128), F32),
        V((2, 128), F32),
        V((TILES, 2, 128), F32),
        V((2, 128, HALF * 128), BF16),
        V((2, HALF * 128, 128), BF16),
        V((2, 3 * 128, 128), BF16),
        V((2, 16, 128), F32),
        V((2, 16, 128), I32),
        V((5, 48, 128), I32),
        V((2, 48, 128), F32),
        V((48, 128), F32),
        V((48, 128), F32),
        V((128, 128), F32),
        V((48, 128), F32),
        V((48, 128), F32),
        V((8, 128), F32),
        V((8, 128), F32),
        V((8, 128), F32),
        V((32, 128), F32),
        V((2, 2, 24, 128), F32),
        V((2, 2, 24, 128), F32),
        V((2, 16, 128), F32),
        V((2, 16, 128), F32),
        V((2, 2, 2, 8, 128), F32),
        V((2, 2, 2, 8, 128), F32),
        V((8, 128), F32),
        DMA((9,)), DMA, DMA((2,)), DMA((2, 2)), DMA((2, 2)), DMA((2,)), DMA((2,)), DMA((2, 2)), DMA((2, 2)), DMA((3,)), DMA((3,)), DMA, DMA,
    ]
    outs = (
        jax.ShapeDtypeStruct((SEC, 2, 8, 128), F32),
        jax.ShapeDtypeStruct((SEC, 2, LENS), F32),
    )
    return pl.pallas_call(
        kernel,
        out_shape=outs,
        in_specs=[hbm] * 9,
        out_specs=(vmem, vmem),
        scratch_shapes=scratch,
        compiler_params=pltpu.CompilerParams(
            collective_id=0, has_side_effects=True
        ),
        name="relax",
    )(displacement, lens_coef, stiff_class, stiff_table, *lists, match_offset)


def solution(mesh):
    in_specs = (
        P("stack", None, "tile", None),
        P("stack", None, None),
        P("stack", "tile", None),
        P(),
        P(("stack", "tile")),
        P(("stack", "tile"), None),
        P(("stack", "tile")),
        P(("stack", "tile")),
        P(None, ("stack", "tile")),
    )
    out_specs = (P("stack", None, "tile", None), P("stack", None, None))
    return jax.shard_map(on_device, mesh=mesh, in_specs=in_specs, out_specs=out_specs, check_vma=False)
```

```python
import functools

import jax
import jax.numpy as jnp
import numpy as np
from jax import lax
from jax.experimental import pallas as pl
from jax.experimental.pallas import tpu as pltpu
from jax.sharding import PartitionSpec as P

ITERS = 4
STEP_RATE = 0.04
LENS_RATE = 4.0
MESH = pl.DeviceIdType.MESH
F32, BF16, I32 = jnp.float32, jnp.bfloat16, jnp.int32

SEC, EXT = 8, 9
TILES, STACKS = 64, 4
HALF = 12
GROW = 48
LENS = 8

NEAR = [(dx, dc) for dx in (2, 1, 3, 0) for dc in (1, 0)]
STEPS = [(dr, dc, 1.0 if dr == 0 or dc == 0 else 0.5) for dr in (-1, 0, 1) for dc in (-1, 0, 1) if dr or dc]


def iota(shape, dim):
    return lax.broadcasted_iota(I32, shape, dim)


def split(x):
    high = x.astype(BF16).astype(F32)
    return high, x - high


def rowpos(side, comp, i):
    return side * 24 + (comp * 8 + i if i < 8 else 16 + comp * 4 + i - 8)


def fold(x):
    for step in (8, 16, 32, 64):
        x = x + pltpu.roll(x, step, 1)
    return x


def along_lanes(source, lanes):
    dims = lax.GatherDimensionNumbers(
        offset_dims=(), collapsed_slice_dims=(1,), start_index_map=(1,),
        operand_batching_dims=(0,), start_indices_batching_dims=(0,),
    )
    return lax.gather(
        source, lanes[:, :, None], dims, slice_sizes=(1, 1), mode=lax.GatherScatterMode.PROMISE_IN_BOUNDS
    )


def pack_rows(a, b):
    last = jnp.where(iota((8, 128), 0) < 4, a[8:16], pltpu.roll(b[8:16], 4, 0))
    return jnp.concatenate([a[0:8], b[0:8], last], axis=0)


def kernel(
    disp_in, lens_in, scls_in, stab_in, msrc_in, mown_in, mdst_in, mlev_in, moff_in,
    dout, cout,
    lens, scls, stab, msrc, mown, mdst, mlev, moff,
    D, K, W, WS, S, F, msg, box, gmsg, ebox, CH, CHT, COS, L, rowix, slotix, basis, offs, base, tin, pull, lval, C, G, tmp, wrow,
    hs, hr, khs, khr, ys, yr, cy,
    in_sem, a_send, a_recv, h_send, h_recv, k_send, k_recv, y_send, y_recv, s_send, s_recv, e_send, e_recv,
):
    t = lax.axis_index("tile")
    g = lax.axis_index("stack")
    z, a = lax.div(t, 8), lax.rem(t, 8)
    x, c = lax.div(a, 2), lax.rem(a, 2)
    up_g, down_g = lax.rem(g + 1, STACKS), lax.rem(g + STACKS - 1, STACKS)
    up_t, down_t = lax.rem(t + 1, TILES), lax.rem(t + TILES - 1, TILES)

    def peer(dz, dx, dc):
        pz, px, pc = lax.rem(z + dz, 8), lax.rem(x + dx, 4), lax.rem(c + dc, 2)
        return pz * 8 + px * 2 + pc

    def each_peer(do):
        def along_z(k, carry):
            odd = lax.rem(k, 2)
            dz = 4 + lax.div(k, 2) - odd * (k)
            for dx, dc in NEAR:
                do(peer(dz, dx, dc))
            return carry

        lax.fori_loop(0, 7, along_z, 0)
        for dx, dc in NEAR:
            if dx or dc:
                do(peer(0, dx, dc))

    loads = [
        pltpu.make_async_copy(src, dst, in_sem.at[n])
        for n, (src, dst) in enumerate((
            (mown_in, mown), (msrc_in, msrc), (mdst_in, mdst), (mlev_in, mlev), (moff_in, moff),
            (disp_in, D.at[pl.ds(0, SEC)]), (scls_in, scls), (lens_in, lens), (stab_in, stab),
        ))
    ]
    for copy in loads:
        copy.start()
    barrier = pltpu.get_barrier_semaphore()

    def greet(p):
        pl.semaphore_signal(barrier, inc=1, device_id={"tile": p}, device_id_type=MESH)

    each_peer(greet)
    for other in (up_g, down_g):
        pl.semaphore_signal(barrier, inc=1, device_id={"stack": other}, device_id_type=MESH)

    def send_rows(par):
        def one(p):
            pltpu.make_async_remote_copy(
                src_ref=msg.at[p], dst_ref=box.at[par, t], send_sem=a_send, recv_sem=a_recv.at[par],
                device_id={"tile": p}, device_id_type=MESH,
            ).start()

        each_peer(one)
        box[par, t] = msg[t]

    def wait_rows(par):
        got = box.at[par, pl.ds(0, TILES - 1)]
        pltpu.make_async_copy(got, got, a_recv.at[par]).wait()
        sent = msg.at[pl.ds(0, TILES - 1)]
        pltpu.make_async_copy(sent, sent, a_send).wait()

    def y_copy(src, dst, sems, recv, index, other):
        return pltpu.make_async_remote_copy(
            src_ref=src, dst_ref=dst, send_sem=sems.at[index], recv_sem=recv.at[index],
            device_id={"stack": other}, device_id_type=MESH,
        )

    def t_copy(src, dst, send, recv, other):
        return pltpu.make_async_remote_copy(
            src_ref=src, dst_ref=dst, send_sem=send, recv_sem=recv,
            device_id={"tile": other}, device_id_type=MESH,
        )

    lane8 = iota((8, 128), 1)
    sub8 = iota((8, 128), 0)
    group8 = lax.shift_right_logical(lane8, 3) - GROW // 8
    own_group = group8 == sub8

    for copy in loads[0:5]:
        copy.wait()
    own = mown[...]
    tri_r, tri_c = iota((128, 256), 0), iota((128, 256), 1)
    tri = jnp.where(tri_r <= tri_c, 1.0, 0.0).astype(BF16)
    lane_own = iota((TILES, 128), 0)
    before = jnp.zeros((TILES, 128), F32)
    src, dst, lev = msrc[...], mdst[...], mlev[...]
    srow, scol = lax.shift_right_logical(src, 7), src & 127
    drow, dcol = lax.shift_right_logical(dst, 7), dst & 127
    live = jnp.where(srow + g * 64 >= STACKS * 64 - 8, 0, lev)
    ints = [v.astype(F32) for v in (srow, scol, drow, dcol, live)]
    slots = jnp.zeros((11 * 16, 128), F32)
    for j in range(8):
        own_j = own[j : j + 1]
        hot = jnp.where(lane_own == own_j, 1.0, 0.0)
        counted = jnp.dot(hot.astype(BF16), tri, preferred_element_type=F32)
        rank = jnp.sum(hot * (counted[:, :128] + before), axis=0, keepdims=True) - 1.0
        before = before + counted[:, 128:]
        rank = rank.astype(I32)
        high = jnp.where(rank >= HALF, 1, 0)
        row_hot = iota((16, 128), 0) == rank - HALF * high
        slot_hot = jnp.where(iota((128, 128), 0) == own_j + TILES * high, 1.0, 0.0).astype(BF16)
        values = [v[j : j + 1] for v in ints]
        for comp in range(2):
            off = moff[comp : comp + 1, j * 128 : (j + 1) * 128]
            first, rest = split(off)
            second, third = split(rest)
            values += [first, second, third]
        picked = jnp.concatenate([jnp.where(row_hot, v, 0.0) for v in values], axis=0).astype(BF16)
        slots = slots + lax.dot_general(picked, slot_hot, (((1,), (1,)), ((), ())), preferred_element_type=F32)
    sl = [slots[16 * v : 16 * v + 16] for v in range(11)]
    mine = sl[0:5] + [sl[5] + sl[6] + sl[7], sl[8] + sl[9] + sl[10]]

    tin[...] = jnp.zeros_like(tin)
    tin[0:112] = jnp.concatenate(mine, axis=0)
    turned = tin[...].T
    msg[:, 0, :] = turned[0:TILES]
    msg[:, 1, :] = turned[TILES:]

    pl.semaphore_wait(barrier, TILES - 1 + 2)
    send_rows(0)

    for copy in loads[5:]:
        copy.wait()
    cls = scls[...]
    stiff = jnp.zeros(cls.shape, F32)
    for k in range(4):
        stiff = jnp.where(cls == k, stab[k], stiff)
    K[0:SEC] = stiff
    C[...] = jnp.zeros_like(C)
    tmp[...] = jnp.zeros_like(tmp)
    for comp in range(2):
        tmp[:, 0:LENS] = lens[:, comp, :]
        wide = fold(tmp[...])
        C[comp : comp + 1] = jnp.sum(jnp.where(own_group, wide, 0.0), axis=0, keepdims=True)

    first = [
        y_copy(D.at[0], D.at[SEC], s_send, s_recv, 0, down_g),
        y_copy(K.at[0], K.at[SEC], s_send, s_recv, 1, down_g),
        y_copy(C, cy, s_send, s_recv, 2, down_g),
    ]
    for copy in first:
        copy.start()

    peer_row = (iota((16, 128), 1) & (TILES - 1)) * 8
    own_row0 = t * 8

    def node_tables(side, values):
        sr, sc, dr, dc = [v.astype(I32) for v in values[0:4]]
        sec = lax.shift_right_logical(sr, 3)
        own_row = sr if side == 0 else sec * 8 + 8 + dr
        own_col = sc if side == 0 else dc
        rowix[side] = own_row
        at = slice(24 * side, 24 * side + 24)
        for n, v in enumerate((own_row, own_col, sec, sc, dc)):
            slotix[n, at] = pack_rows(v, v)
        for i in range(HALF):
            at = slice(i * 128, (i + 1) * 128)
            CH[side, :, at] = jnp.where(iota((128, 128), 0) == own_col[i : i + 1], 1.0, 0.0).astype(BF16)

    def pull_tables(side, values):
        sr, dr = values[0].astype(I32), values[2].astype(I32)
        ox, oy = values[5], values[6]
        sign = 1.0 if side == 0 else -1.0
        s_in = sr & 7
        ysrc = (own_row0 if side == 0 else peer_row) + s_in
        ydst = (peer_row if side == 0 else own_row0) + dr
        ramp_s = (1.0 + ysrc.astype(F32) * (2.0 / 512)) * sign
        ramp_d = (1.0 + ydst.astype(F32) * (2.0 / 512)) * -sign
        weight = values[4] * 0.125
        at = slice(24 * side, 24 * side + 24)
        offs[at] = pack_rows(ox, oy) * sign
        base[at] = pack_rows(weight, weight)
        for end, ramp in ((0, ramp_s), (1, ramp_d)):
            wide = pack_rows(ramp, ramp)
            for k in range(LENS):
                turn = (k * slotix[3 + end, at]) & 255
                basis[end, k, at] = wide * jnp.cos(turn.astype(F32) * (np.pi / 128))
        own_col = (values[1] if side == 0 else values[3]).astype(I32)
        for i in range(HALF):
            hot = jnp.where(iota((128, 128), 0) == own_col[i : i + 1], 1.0, 0.0)
            CHT[side, i * 128 : (i + 1) * 128] = hot.T.astype(BF16)

    def gather(side, first, count):
        d_hi, d_lo = split(D[first : first + count].reshape(count * 16, 128))
        both = jnp.concatenate([d_hi, d_lo], axis=1).astype(BF16)
        for n in range(HALF // 2):
            hot = CH[side, :, n * 256 : (n + 1) * 256]
            got = jnp.dot(both, jnp.concatenate([hot, hot], axis=0), preferred_element_type=F32)
            for m in range(2):
                i = 2 * n + m
                row = rowix[side, i : i + 1]
                sec, within = lax.shift_right_logical(row, 3), row & 7
                at = slice(m * 128, (m + 1) * 128)
                total = [jnp.zeros((8, 128), F32), jnp.zeros((8, 128), F32)]
                for s in range(count):
                    hit = sec == s + first
                    for comp in range(2):
                        r = (s * 2 + comp) * 8
                        total[comp] = jnp.where(hit, got[r : r + 8, at], total[comp])
                for comp in range(2):
                    value = jnp.sum(jnp.where(sub8 == within, total[comp], 0.0), axis=0, keepdims=True)
                    r = rowpos(side, comp, i)
                    tin[r : r + 1] = value

    def by_comp(rows):
        wide = [jnp.broadcast_to(row, (8, 128)) for row in rows]
        return wide + [jnp.where(sub8 < 4, wide[0], wide[1])]

    def gather_edge(side):
        edge = side * SEC
        blocks = [slice(24 * side + 8 * q, 24 * side + 8 * q + 8) for q in range(3)]
        total = [jnp.zeros((8, 128), F32)] * 3
        for r in range(8):
            for q, source in enumerate(by_comp([D[edge, comp, r : r + 1] for comp in range(2)])):
                found = along_lanes(source, slotix[1, blocks[q]])
                total[q] = jnp.where(slotix[0, blocks[q]] == edge * 8 + r, found, total[q])
        for q in range(3):
            tin[blocks[q]] = tin[blocks[q]] + total[q]

    def exchange(par):
        turned = tin[...].T
        flat = msg.reshape(128, 128)
        for comp in range(2):
            flat[pl.ds(comp, TILES, stride=2), :] = turned[comp * TILES : (comp + 1) * TILES] + G[comp : comp + 1]
        send_rows(par)

    node_tables(0, mine)
    tin[...] = jnp.zeros_like(tin)
    gather(0, 0, SEC)
    pull_tables(0, mine)
    for n in range(2):
        k = (iota((128, 128), 1 - n) - GROW) & 7
        turn = (iota((128, 128), n) * k) & 255
        high, low = split(jnp.cos(turn.astype(F32) * (np.pi / 128)))
        COS[n] = jnp.concatenate([high, high, low], axis=0).astype(BF16)
    group16 = lax.shift_right_logical(iota((16, 128), 1), 3) - GROW // 8
    mask72 = iota((EXT * LENS, 128), 1) - GROW == iota((EXT * LENS, 128), 0)
    mask16 = (group16 == iota((16, 128), 0)) & (group16 < EXT)

    for copy in first:
        copy.wait()
    for comp in range(2):
        C[comp : comp + 1] = C[comp : comp + 1] + jnp.where(
            group8[0:1] == SEC, pltpu.roll(cy[comp : comp + 1], LENS * SEC, 1), 0.0
        )
    hs[...] = jnp.zeros_like(hs)
    khs[...] = jnp.zeros_like(khs)

    def beside(par):
        return [
            t_copy(hs.at[par, 0], hr.at[par, 1], h_send.at[par, 0], h_recv.at[par, 1], down_t),
            t_copy(hs.at[par, 1], hr.at[par, 0], h_send.at[par, 1], h_recv.at[par, 0], up_t),
        ]

    def send_beside(par):
        for s in range(EXT):
            for comp in range(2):
                r = s * 2 + comp
                hs[par, 0, r : r + 1] = D[s, comp, 0:1]
                hs[par, 1, r : r + 1] = D[s, comp, 7:8]
        for copy in beside(par):
            copy.start()

    for s in range(EXT):
        khs[0, s : s + 1] = K[s, 0:1]
        khs[1, s : s + 1] = K[s, 7:8]
    kcopies = [
        t_copy(khs.at[0], khr.at[1], k_send.at[0], k_recv.at[1], down_t),
        t_copy(khs.at[1], khr.at[0], k_send.at[1], k_recv.at[0], up_t),
    ]
    for copy in kcopies:
        copy.start()
    send_beside(0)

    def shifted(v, low, high):
        above = jnp.where(sub8 == 0, low, pltpu.roll(v, 1, 0))
        below = jnp.where(sub8 == 7, high, pltpu.roll(v, 7, 0))
        for dr, row in ((-1, above), (0, v), (1, below)):
            for dc in (-1, 0, 1):
                if dr or dc:
                    yield row if dc == 0 else pltpu.roll(row, 1 if dc < 0 else 127, 1)

    def turn_rows(par):
        flat = box.at[par].reshape(128, 128)
        both = jnp.concatenate([flat[pl.ds(n, TILES, stride=2), :] for n in range(2)], axis=0)
        return both, both.T

    wait_rows(0)
    _, theirs = turn_rows(0)
    yours = [theirs[16 * v : 16 * v + 16] for v in range(7)]
    node_tables(1, yours)
    gather(1, 1, SEC)
    G[...] = jnp.zeros_like(G)
    exchange(1)
    pull_tables(1, yours)
    for copy in kcopies:
        copy.wait()
    has_low, has_high = jnp.where(t > 0, 1.0, 0.0), jnp.where(t < TILES - 1, 1.0, 0.0)
    for s in range(EXT):
        v = K[s]
        total = jnp.zeros((8, 128), F32)
        near = shifted(v, khr[0, s : s + 1] * has_low, khr[1, s : s + 1] * has_high)
        for n, ((dr, dc, scale), other) in enumerate(zip(STEPS, near)):
            w = scale * jnp.minimum(v, other)
            if dc:
                w = jnp.where(lane8 == (0 if dc < 0 else 127), 0.0, w)
            W[n, s] = w
            total = total + w
        WS[s] = total

    wrow[...] = jnp.zeros_like(wrow)

    ramp8 = 1.0 + (own_row0 + sub8).astype(F32) * (2.0 / 512)
    lens_step = LENS_RATE * SEC / (1024 * TILES)

    def take_gradient(both):
        for comp in range(2):
            total = jnp.sum(both[comp * TILES : (comp + 1) * TILES], axis=0, keepdims=True)
            C[comp : comp + 1] = C[comp : comp + 1] + lens_step * jnp.where(group8[0:1] >= 0, total, 0.0)

    def lens_values():
        rows = []
        for comp in range(2):
            wide = jnp.broadcast_to(C[comp : comp + 1], (EXT * LENS, 128))
            rows.append(jnp.where(mask72, wide, 0.0))
        c_hi, c_lo = split(jnp.concatenate(rows, axis=0))
        cat = jnp.concatenate([c_hi, c_lo], axis=1).astype(BF16)
        ones = jnp.ones((256, 128), BF16)
        L[...] = jnp.dot(cat, ones, preferred_element_type=F32).reshape(2, EXT * LENS, 128)
        blocks = [slice(8 * b, 8 * b + 8) for b in range(6)]
        hits = [[slotix[2, blocks[b]] == s for s in range(1, SEC)] for b in range(6)]
        total = [jnp.zeros((8, 128), F32)] * 6
        for end in range(2):
            for k in range(LENS):
                coefs = []
                for s in range(SEC):
                    at = (s + end) * LENS + k
                    coefs.append(by_comp([L[comp, at : at + 1] for comp in range(2)]))
                for b in range(6):
                    coef = coefs[0][b % 3]
                    for s in range(1, SEC):
                        coef = jnp.where(hits[b][s - 1], coefs[s][b % 3], coef)
                    total[b] = total[b] + coef * basis[end, k, blocks[b]]
        for b in range(6):
            lval[blocks[b]] = total[b]

    def forces(theirs):
        other = jnp.concatenate([theirs[24:48], theirs[0:24]], axis=0)
        r = tin[0:48] - other + offs[...] + lval[...]
        sq = r * r
        for side in range(2):
            b = side * 24
            near = sq[b : b + 8] + sq[b + 8 : b + 16]
            last = sq[b + 16 : b + 24]
            last = last + pltpu.roll(last, 4, 0)
            size = jnp.concatenate([near, near, last], axis=0)
            pull[b : b + 24] = -base[b : b + 24] * r[b : b + 24] / (1.0 + size * 0.25)

    def scatter(side, first, count):
        rows = iota((count * 8, 128), 0) + first * 8
        total = jnp.zeros((4 * count * 8, 128), F32)
        for n in range(HALF // 2):
            cols = []
            for m in range(2):
                i = 2 * n + m
                hit = rows == rowix[side, i : i + 1]
                pieces = []
                for comp in range(2):
                    r = rowpos(side, comp, i)
                    pieces += list(split(pull[r : r + 1]))
                cols.append(jnp.concatenate([jnp.where(hit, p, 0.0) for p in pieces], axis=0))
            spread = jnp.concatenate(cols, axis=1).astype(BF16)
            total = total + jnp.dot(
                spread, CHT[side, n * 256 : (n + 1) * 256], preferred_element_type=F32
            )
        total = total.reshape(2, 2, count, 8, 128)
        return [total[comp, 0] + total[comp, 1] for comp in range(2)]

    def springs(par):
        for s in range(EXT):
            for comp in range(2):
                r = s * 2 + comp
                v = D[s, comp]
                total = -WS[s] * v
                near = shifted(v, hr[par, 0, r : r + 1], hr[par, 1, r : r + 1])
                for n, other in enumerate(near):
                    total = total + W[n, s] * other
                S[s, comp] = total

    def ramp_sums(sections):
        for s in sections:
            for comp in range(2):
                r = comp * 16 + s
                wrow[r : r + 1] = jnp.sum(ramp8 * F[s, comp], axis=0, keepdims=True)

    def gradient():
        w_hi, w_lo = split(wrow[...])
        cat = jnp.concatenate([w_hi, w_lo, w_hi], axis=1).astype(BF16)
        out = jnp.dot(cat, COS[0], preferred_element_type=F32)
        for comp in range(2):
            G[comp : comp + 1] = jnp.sum(
                jnp.where(mask16, out[comp * 16 : comp * 16 + 16], 0.0), axis=0, keepdims=True
            )

    def arrive(it):
        par = lax.rem(it + 1, 2)
        hpar = lax.rem(it, 2)
        for copy in beside(hpar):
            copy.wait()
        springs(hpar)
        wait_rows(par)
        both, theirs = turn_rows(par)
        take_gradient(both)
        lens_values()
        forces(theirs)
        for side, edge in ((1, SEC), (0, 0)):
            on_edge = scatter(side, edge, 1)
            for comp in range(2):
                F[edge, comp] = on_edge[comp][0]
            ys[hpar, 1 - side] = F[edge]
        copies = [y_pair(hpar, 0, up_g), y_pair(hpar, 1, down_g)]
        for copy in copies:
            copy.start()
        return par, hpar, copies

    def inner_forces():
        inner = [scatter(side, 1, SEC - 1) for side in range(2)]
        for comp in range(2):
            F[1:SEC, comp] = inner[0][comp] + inner[1][comp]
        ramp_sums(range(1, SEC))

    def sweep(it, carry):
        par, hpar, copies = arrive(it)
        inner_forces()
        D[1:SEC] = D[1:SEC] + STEP_RATE * (S[1:SEC] + F[1:SEC])
        gather(0, 1, SEC - 1)
        gather(1, 1, SEC - 1)
        for copy in copies:
            copy.wait()
        for way, edge in ((0, 0), (1, SEC)):
            F[edge] = F[edge] + yr[hpar, way]
            D[edge] = D[edge] + STEP_RATE * (S[edge] + F[edge])
        ramp_sums((0, SEC))
        gradient()

        gather_edge(0)
        gather_edge(1)
        exchange(1 - par)
        send_beside(1 - hpar)
        return carry

    def y_pair(par, way, other):
        return pltpu.make_async_remote_copy(
            src_ref=ys.at[par, way], dst_ref=yr.at[par, way], send_sem=y_send.at[par, way],
            recv_sem=y_recv.at[par, way], device_id={"stack": other}, device_id_type=MESH,
        )

    lax.fori_loop(0, ITERS - 1, sweep, 0)

    last, lpar, copies = arrive(ITERS - 1)
    inner_forces()
    ramp_sums((0, SEC))
    gradient()
    gmsg[...] = G[0:2]
    fin = 1 - last

    def send_gradient(p):
        pltpu.make_async_remote_copy(
            src_ref=gmsg, dst_ref=box.at[fin, t], send_sem=a_send, recv_sem=a_recv.at[fin],
            device_id={"tile": p}, device_id_type=MESH,
        ).start()

    def send_edge(p):
        pltpu.make_async_remote_copy(
            src_ref=gmsg, dst_ref=ebox.at[t], send_sem=e_send, recv_sem=e_recv,
            device_id={"stack": up_g, "tile": p}, device_id_type=MESH,
        ).start()

    def send_both(p):
        send_edge(p)
        send_gradient(p)

    each_peer(send_both)
    send_edge(t)
    box[fin, t] = gmsg[...]
    for copy in copies:
        copy.wait()
    F[0] = F[0] + yr[lpar, 0]
    dout[...] = D[0:SEC] + STEP_RATE * (S[0:SEC] + F[0:SEC])
    wait_rows(fin)
    pltpu.make_async_copy(ebox, ebox, e_recv).wait()
    pltpu.make_async_copy(ebox, ebox, e_send).wait()
    for comp in range(2):
        total = jnp.sum(box[fin, :, comp, :], axis=0, keepdims=True)
        below = jnp.sum(ebox[:, comp, :], axis=0, keepdims=True)
        below = pltpu.roll(below, 128 - LENS * SEC, 1)
        first = jnp.where(group8[0:1] == 0, below, 0.0)
        total = jnp.where((group8[0:1] >= 0) & (group8[0:1] < SEC), total + first, 0.0)
        C[comp : comp + 1] = C[comp : comp + 1] + lens_step * total
    for comp in range(2):
        wide = fold(jnp.where(own_group, jnp.broadcast_to(C[comp : comp + 1], (8, 128)), 0.0))
        cout[:, comp, :] = wide[:, 0:LENS]


def on_device(displacement, lens_coef, stiff_class, stiff_table, match_src, match_owner, match_dst, match_level, match_offset):
    vmem = pl.BlockSpec(memory_space=pltpu.VMEM)
    hbm = pl.BlockSpec(memory_space=pltpu.HBM)
    V, DMA = pltpu.VMEM, pltpu.SemaphoreType.DMA
    lists = [a.reshape(8, 128) for a in (match_src, match_owner, match_dst, match_level)]
    scratch = [
        V((SEC, 2, LENS), F32),
        V((SEC, 8, 128), I32),
        pltpu.SMEM((4,), F32),
        V((8, 128), I32), V((8, 128), I32), V((8, 128), I32), V((8, 128), I32),
        V((2, 1024), F32),
        V((EXT, 2, 8, 128), F32),
        V((EXT, 8, 128), F32),
        V((8, EXT, 8, 128), F32),
        V((EXT, 8, 128), F32),
        V((EXT, 2, 8, 128), F32),
        V((EXT, 2, 8, 128), F32),
        V((TILES, 2, 128), F32),
        V((2, TILES, 2, 128), F32),
        V((2, 128), F32),
        V((TILES, 2, 128), F32),
        V((2, 128, HALF * 128), BF16),
        V((2, HALF * 128, 128), BF16),
        V((2, 3 * 128, 128), BF16),
        V((2, EXT * LENS, 128), F32),
        V((2, 16, 128), I32),
        V((5, 48, 128), I32),
        V((2, LENS, 48, 128), F32),
        V((48, 128), F32),
        V((48, 128), F32),
        V((128, 128), F32),
        V((48, 128), F32),
        V((48, 128), F32),
        V((8, 128), F32),
        V((8, 128), F32),
        V((8, 128), F32),
        V((32, 128), F32),
        V((2, 2, 24, 128), F32),
        V((2, 2, 24, 128), F32),
        V((2, 16, 128), F32),
        V((2, 16, 128), F32),
        V((2, 2, 2, 8, 128), F32),
        V((2, 2, 2, 8, 128), F32),
        V((8, 128), F32),
        DMA((9,)), DMA, DMA((2,)), DMA((2, 2)), DMA((2, 2)), DMA((2,)), DMA((2,)), DMA((2, 2)), DMA((2, 2)), DMA((3,)), DMA((3,)), DMA, DMA,
    ]
    outs = (
        jax.ShapeDtypeStruct((SEC, 2, 8, 128), F32),
        jax.ShapeDtypeStruct((SEC, 2, LENS), F32),
    )
    return pl.pallas_call(
        kernel,
        out_shape=outs,
        in_specs=[hbm] * 9,
        out_specs=(vmem, vmem),
        scratch_shapes=scratch,
        compiler_params=pltpu.CompilerParams(
            collective_id=0, has_side_effects=True
        ),
        name="relax",
    )(displacement, lens_coef, stiff_class, stiff_table, *lists, match_offset)


def solution(mesh):
    in_specs = (
        P("stack", None, "tile", None),
        P("stack", None, None),
        P("stack", "tile", None),
        P(),
        P(("stack", "tile")),
        P(("stack", "tile"), None),
        P(("stack", "tile")),
        P(("stack", "tile")),
        P(None, ("stack", "tile")),
    )
    out_specs = (P("stack", None, "tile", None), P("stack", None, None))
    return jax.shard_map(on_device, mesh=mesh, in_specs=in_specs, out_specs=out_specs, check_vma=False)
```
